32 devices in a mesh: slab: 2 (over x), line: 8 (over z, y), band: 2 (over core).
Axes of the slice: x: 2, y: 2, z: 4, core: 2. Of those that a mesh axis runs over, the one named last changes fastest.
Arguments:
- cube: bfloat16 [230, 2048, 256], P('band', ('slab', 'line')), parts along dimension 1, may hold values from -6 to 6
- observed: bfloat16 [13, 2048, 256], P(None, ('slab', 'line')), parts along dimension 1, may hold values from -6 to 6
- along_kernels: bfloat16 [3, 128, 128], replicated, may hold values from -0.3125 to 0.3125
- along_offsets: int32 [3], replicated, may hold values from -1 to 1, as said below
- across_kernels: bfloat16 [3, 128, 128], replicated, may hold values from -0.3125 to 0.3125
- across_offsets: int32 [3], replicated, may hold values from -1 to 1, as said below
- resp_start: int32 [13], replicated, may hold values from 0 to 21
- resp_values: bfloat16 [13, 20], replicated, may hold values from 0.049804688 to 0.3984375
Outputs:
- synthetic: float32 [13, 2048, 256], P(None, ('slab', 'line')), parts along dimension 1
- angles: float32 [2048, 256], P(('slab', 'line')), parts along dimension 0
The draws below stay inside these ranges and needn't reach their ends.
There are 2 independent parts, one for each index of `slab`. The reference program is written for one: setup_inputs(seed, part) draws one part's arguments, and reference() takes and returns one part's arrays. A program takes and returns all parts, laid end to end along the dimension named above; an argument that names none is the same for every part. Nothing has to cross between parts.
Inputs may be any that keep to these rules, and one draw needn't show every extreme that they name: `along_offsets`: the three entries are -1, 0 and 1, each once. `across_offsets`: the three entries are -1, 0 and 1, each once.
All inputs are finite; a program needn't handle non-finite values.
Results may differ from the reference program's by a relative error of at most 0.0003.
Values may be sent and summed in bfloat16 or wider, within the bound.
A program may use at most 192 MiB of HBM per device.

```python
import jax
import jax.numpy as jnp
from jax import lax

BANDS = 230
MS = 13
BLK = 128
SPB = 10
COLS = 256
LINES = 1024
NSB = 23


def draw_along_offsets(key, part):
    return (jax.random.permutation(jax.random.fold_in(key, 11), 3) - 1).astype(jnp.int32)


def draw_across_offsets(key, part):
    return (jax.random.permutation(jax.random.fold_in(key, 23), 3) - 1).astype(jnp.int32)


def place_ends(entries, rng, low, high):
    longest = entries.shape.index(max(entries.shape))
    spots = []
    for shift in (0, 1):
        where = [jax.random.randint(jax.random.fold_in(rng, axis), (), 0, length) for axis, length in enumerate(entries.shape)]
        where[longest] = (where[longest] + shift) % entries.shape[longest]
        spots.append(tuple(where))
    return entries.at[spots[0]].set(low).at[spots[1]].set(high)


def level_of(key, dims, shards, low, high):
    factor_of = 1.0
    for dim, shards_of in shards:
        heights = jax.random.uniform(jax.random.fold_in(jax.random.fold_in(key, 6), dim), (shards_of,), jnp.float32, low / len(shards), high / len(shards))
        factor_of = factor_of * jnp.repeat(jnp.exp(heights), dims[dim] // shards_of).reshape((-1,) + (1,) * (len(dims) - 1 - dim))
    return factor_of


def bell_draw(rng, dims, scale, reach, shards=(), held_as=jnp.bfloat16):
    entries = jax.random.normal(rng, dims, jnp.float32) * scale
    if len(shards) > 0:
        entries = level_of(rng, dims, shards, -0.22, 0.18) * entries
    return jnp.clip(entries, min=-reach, max=reach).astype(held_as)


def setup_inputs(seed: int = 0, part: int = 0) -> dict:
    key_list = jax.random.split(jax.random.key(seed), 9)
    own_keys = jax.random.split(jax.random.fold_in(key_list[8], part), 9)
    cube = bell_draw(own_keys[0], (BANDS, LINES, COLS), 1.0, 6.0, ((0, 2), (1, 8)))
    observed = bell_draw(own_keys[1], (MS, LINES, COLS), 1.0, 6.0, ((1, 8),))
    along_kernels = bell_draw(key_list[2], (3, BLK, BLK), (3 * BLK) ** -0.5, 0.3125)
    along_offsets = draw_along_offsets(jax.random.fold_in(key_list[8], 71), part)
    across_kernels = bell_draw(key_list[4], (3, BLK, BLK), (3 * BLK) ** -0.5, 0.3125)
    across_offsets = draw_across_offsets(jax.random.fold_in(key_list[8], 71), part)
    resp_start = place_ends(jax.random.randint(key_list[6], (MS,), 0, NSB - 1), jax.random.fold_in(key_list[6], 1), 0, (NSB - 1) - 1).astype(jnp.int32)
    resp_values = jnp.clip(jax.random.uniform(key_list[7], (MS, 2 * SPB), jnp.float32, 0.049804688, 0.3984375), 0.049804688, 0.3984375).astype(jnp.bfloat16)
    return {"cube": cube, "observed": observed, "along_kernels": along_kernels, "along_offsets": along_offsets, "across_kernels": across_kernels, "across_offsets": across_offsets, "resp_start": resp_start, "resp_values": resp_values}


def pick_kernels(kernels, offsets):
    shifts = jnp.arange(3, dtype=jnp.int32) - 1
    onehot = (offsets[None, :] == shifts[:, None]).astype(jnp.float32)
    return jnp.einsum('sk,kpq->spq', onehot, kernels.astype(jnp.float32), precision=lax.Precision.HIGHEST)

def dense_response(resp_start, resp_values):
    bands = jnp.arange(BANDS, dtype=jnp.int32)
    local = bands[None, :] - SPB * resp_start[:, None]
    slots = jnp.arange(2 * SPB, dtype=jnp.int32)
    hits = local[:, :, None] == slots[None, None, :]
    return lax.optimization_barrier(jnp.sum(jnp.where(hits, resp_values.astype(jnp.float32)[:, None, :], jnp.float32(0.0)), axis=-1))

def along_filter(field, chosen):
    count = field.shape[1] // BLK
    blocks = field.astype(jnp.float32).reshape(field.shape[0], count, BLK, field.shape[2])
    padded = jnp.pad(blocks, ((0, 0), (1, 1), (0, 0), (0, 0)))
    total = jnp.zeros(blocks.shape, jnp.float32)
    for index in range(3):
        total = total + jnp.einsum('pq,bnqc->bnpc', chosen[index], padded[:, index:index + count], precision=lax.Precision.HIGHEST)
    return total.reshape(field.shape)

def across_filter(field, chosen):
    count = field.shape[2] // BLK
    blocks = field.astype(jnp.float32).reshape(field.shape[0], field.shape[1], count, BLK)
    padded = jnp.pad(blocks, ((0, 0), (0, 0), (1, 1), (0, 0)))
    total = jnp.zeros(blocks.shape, jnp.float32)
    for index in range(3):
        total = total + jnp.einsum('pq,blnq->blnp', chosen[index], padded[:, :, index:index + count], precision=lax.Precision.HIGHEST)
    return total.reshape(field.shape)

def reference(cube, observed, along_kernels, along_offsets, across_kernels, across_offsets, resp_start, resp_values):
    along_pick = pick_kernels(along_kernels, along_offsets)
    across_pick = pick_kernels(across_kernels, across_offsets)
    response = dense_response(resp_start, resp_values)
    groups = cube.reshape(NSB, SPB, LINES, COLS)
    weights = response.reshape(MS, NSB, SPB).transpose(1, 0, 2)

    def accumulate(carry, item):
        group, weight = item
        along = along_filter(group, along_pick)
        across = across_filter(along, across_pick)
        return (carry + jnp.einsum('mb,blc->mlc', weight, across, precision=lax.Precision.HIGHEST), None)
    start = jnp.zeros((MS, LINES, COLS), jnp.float32)
    synthetic, unused = lax.scan(accumulate, start, (groups, weights))
    seen = observed.astype(jnp.float32)
    inner = lax.optimization_barrier(jnp.sum(synthetic * seen, axis=0))
    first = jnp.sqrt(lax.optimization_barrier(jnp.sum(synthetic * synthetic, axis=0)))
    second = jnp.sqrt(lax.optimization_barrier(jnp.sum(seen * seen, axis=0)))
    angles = jnp.arccos(jnp.clip(inner / jnp.maximum(first * second, 1.0), -1.0, 1.0))
    return (synthetic, angles)
```

```python
import functools
import math

import jax
import jax.numpy as jnp
from jax import lax
from jax.experimental import pallas as pl
from jax.experimental.pallas import tpu as pltpu
from jax.sharding import PartitionSpec as P

BLK = 128
SPB = 10
ROWS = 16
LAG = 2
FIRST = 2
MESH = pl.DeviceIdType.MESH
F32 = jnp.float32
BF16 = jnp.bfloat16


def halves(value):
    high = value.astype(BF16)
    low = (value - high.astype(F32)).astype(BF16)
    return high, low


def picked(kernels, offsets, shift):
    total = None
    for k in range(3):
        term = jnp.where(offsets[k] == shift, kernels[k].astype(F32), 0.0)
        total = term if total is None else total + term
    return total


def iota(shape, dim):
    return lax.broadcasted_iota(jnp.int32, shape, dim)


def kernel(
    sizes,
    cube,
    observed,
    along_hbm,
    across_hbm,
    values_hbm,
    along_off_hbm,
    across_off_hbm,
    start_hbm,
    synthetic,
    cosine,
    folder,
    field,
    seen,
    along,
    across,
    taps,
    mixer,
    given,
    own,
    got,
    total,
    coded,
    scale,
    near,
    near_scale,
    far,
    far_scale,
    result,
    angle_buf,
    values,
    along_off,
    across_off,
    start,
    cube_sem,
    arg_sem,
    give_sem,
    got_sem,
    send_sem,
    near_sem,
    scale_send_sem,
    near_scale_sem,
    pass_sem,
    far_sem,
    scale_pass_sem,
    far_scale_sem,
    share_sem,
    result_sem,
    out_sem,
):
    bands, lines, columns, ms, half, line_size = sizes
    groups = lines // ROWS
    core = lax.axis_index("band")
    index = lax.axis_index("line")
    other = {"band": 1 - core}
    even = index % 2 == 0
    partner = {"line": index + 1 - 2 * (index % 2)}
    step = 2 - 4 * (index % 2)
    ahead, behind = index + step, index - step
    has_ahead = jnp.logical_and(ahead >= 0, ahead < line_size)
    has_behind = jnp.logical_and(behind >= 0, behind < line_size)

    def cube_copy(g):
        return pltpu.make_async_copy(
            cube.at[:, pl.ds(g * ROWS, ROWS), :], field.at[g], cube_sem.at[g]
        )

    along_copy = pltpu.make_async_copy(along_hbm, along, arg_sem.at[0])
    across_copy = pltpu.make_async_copy(across_hbm, across, arg_sem.at[1])
    seen_copy = pltpu.make_async_copy(observed, seen, arg_sem.at[2])
    early = [
        pltpu.make_async_copy(values_hbm, values, arg_sem.at[4]),
        pltpu.make_async_copy(start_hbm, start, arg_sem.at[5]),
        pltpu.make_async_copy(along_off_hbm, along_off, arg_sem.at[6]),
        pltpu.make_async_copy(across_off_hbm, across_off, arg_sem.at[7]),
    ]
    for copy in early:
        copy.start()
    for g in range(FIRST):
        cube_copy(g).start()

    barrier = pltpu.get_barrier_semaphore()
    pl.semaphore_signal(barrier, inc=1, device_id=other, device_id_type=MESH)
    pl.semaphore_signal(barrier, inc=1, device_id=partner, device_id_type=MESH)

    @pl.when(has_ahead)
    def _():
        pl.semaphore_signal(barrier, inc=1, device_id={"line": ahead}, device_id_type=MESH)

    @pl.when(has_behind)
    def _():
        pl.semaphore_signal(barrier, inc=1, device_id={"line": behind}, device_id_type=MESH)

    for copy in early:
        copy.wait()
    for g in range(FIRST, groups):
        cube_copy(g).start()
    along_copy.start()
    across_copy.start()
    seen_copy.start()

    lane = core * bands + iota((ms, 128), 1)
    row = iota((ms, 128), 0)
    first = jnp.zeros((ms, 128), jnp.int32)
    for m in range(ms):
        first = jnp.where(row == m, start[m], first)
    slot = lane - SPB * first
    weights = values[...].astype(F32)
    response = jnp.zeros((ms, 128), F32)
    for j in range(2 * SPB):
        response = jnp.where(slot == j, weights[:, j : j + 1], response)
    tall = 2 * half * ROWS
    picks = iota((tall, ms), 0) // ROWS
    owner = jnp.where(picks < half, (1 - core) * half + picks, core * half + picks - half)
    choose = (owner == iota((tall, ms), 1)).astype(BF16)
    per_row = jnp.dot(choose, response.astype(BF16), preferred_element_type=F32).astype(BF16)
    wide = bands * ROWS
    spread = (iota((128, wide), 1) // ROWS == iota((128, wide), 0)).astype(BF16)
    spread_rows = jnp.dot(per_row, spread, preferred_element_type=F32)
    same = iota((tall, wide), 0) % ROWS == iota((tall, wide), 1) % ROWS
    folder[...] = jnp.where(same, spread_rows, 0.0).astype(BF16)

    peers = 2 + has_ahead.astype(jnp.int32) + has_behind.astype(jnp.int32)
    pl.semaphore_wait(barrier, peers)

    def give_copy(g):
        return pltpu.make_async_remote_copy(
            src_ref=given.at[g],
            dst_ref=got.at[g],
            send_sem=give_sem.at[g],
            recv_sem=got_sem.at[g],
            device_id=other,
            device_id_type=MESH,
        )

    def fold(g, carry):
        cube_copy(g).wait()
        block = field[g].reshape(wide, columns)
        part = jnp.dot(folder[...], block, preferred_element_type=F32)
        part = part.reshape(2 * half, ROWS, columns)
        given[g] = part[:half]
        own[g] = part[half:]
        give_copy(g).start()
        return carry

    lax.fori_loop(0, groups, fold, 0)

    along_copy.wait()
    across_copy.wait()
    before, after = (picked(along, along_off, -1), picked(along, along_off, 1))
    middle = picked(along, along_off, 0)
    near_tap = jnp.where(even, after, before)
    far_tap = jnp.where(even, before, after)
    for slot_index, tap in enumerate((middle, near_tap, far_tap)):
        tap = tap.astype(BF16)
        taps[slot_index] = jnp.concatenate([tap, tap], axis=1)
    count = columns // BLK
    mixer[...] = jnp.zeros(mixer.shape, BF16)
    for shift in (-1, 0, 1):
        turned = jnp.transpose(picked(across, across_off, shift)).astype(BF16)
        for j in range(count):
            if 0 <= j + shift < count:
                for part in range(2):
                    top = part * columns + (j + shift) * BLK
                    mixer[top : top + BLK, j * BLK : (j + 1) * BLK] = turned

    def code_copies(m):
        return (
            pltpu.make_async_remote_copy(
                src_ref=coded.at[m],
                dst_ref=near.at[m],
                send_sem=send_sem.at[m],
                recv_sem=near_sem.at[m],
                device_id=partner,
                device_id_type=MESH,
            ),
            pltpu.make_async_remote_copy(
                src_ref=scale.at[m],
                dst_ref=near_scale.at[m],
                send_sem=scale_send_sem.at[m],
                recv_sem=near_scale_sem.at[m],
                device_id=partner,
                device_id_type=MESH,
            ),
        )

    def pass_copies(m):
        return (
            pltpu.make_async_remote_copy(
                src_ref=near.at[m],
                dst_ref=far.at[m],
                send_sem=pass_sem.at[m],
                recv_sem=far_sem.at[m],
                device_id={"line": ahead},
                device_id_type=MESH,
            ),
            pltpu.make_async_remote_copy(
                src_ref=near_scale.at[m],
                dst_ref=far_scale.at[m],
                send_sem=scale_pass_sem.at[m],
                recv_sem=far_scale_sem.at[m],
                device_id={"line": ahead},
                device_id_type=MESH,
            ),
        )

    def share_copy(m):
        return pltpu.make_async_remote_copy(
            src_ref=result.at[0, m],
            dst_ref=result.at[1, m],
            send_sem=share_sem.at[m],
            recv_sem=result_sem.at[m],
            device_id=other,
            device_id_type=MESH,
        )

    def out_copy(which, m):
        place = core if which == 0 else 1 - core
        return pltpu.make_async_copy(
            result.at[which, m], synthetic.at[place * half + m], out_sem.at[which, m]
        )

    def guard(m, place, body):
        if half + m < ms:
            body()
        else:
            pl.when(place * half + m < ms)(body)

    @pl.when(jnp.logical_not(has_behind))
    def _():
        far[...] = jnp.zeros(far.shape, jnp.int16)
        far_scale[...] = jnp.zeros(far_scale.shape, F32)

    for g in range(groups):
        give_copy(g).wait_recv()

    for m in range(half):

        def encode(m=m):
            value = (own[:, m] + got[:, m]).reshape(lines, columns)
            total[m] = value
            peak = jnp.max(jnp.abs(value), axis=0, keepdims=True)
            inverse = jnp.where(peak > 0.0, 32767.0 / jnp.maximum(peak, 1e-30), 0.0)
            coded[m] = jnp.round(value * inverse).astype(jnp.int32).astype(jnp.int16)
            scale[m] = peak * (1.0 / 32767.0)
            for copy in code_copies(m):
                copy.start()

        guard(m, core, encode)

    seen_copy.wait()

    def filtered(slot_index, value):
        high, low = halves(value)
        stacked = jnp.concatenate([high, low], axis=0)
        return jnp.dot(taps[slot_index], stacked, preferred_element_type=F32)

    def arrive(m):
        copies = code_copies(m)
        for copy in copies:
            copy.wait_recv()

        @pl.when(has_ahead)
        def _():
            for copy in pass_copies(m):
                copy.start()

        total[m] = (
            filtered(0, total[m])
            + filtered(1, near[m].astype(jnp.int32).astype(F32)) * near_scale[m]
        )

    def finish(m):
        @pl.when(has_behind)
        def _():
            for copy in pass_copies(m):
                copy.wait_recv()

        smooth = total[m] + filtered(2, far[m].astype(jnp.int32).astype(F32)) * far_scale[m]
        high, low = halves(smooth)
        both = jnp.concatenate([high, low], axis=1)
        result[0, m] = jnp.dot(both, mixer[...], preferred_element_type=F32)
        share_copy(m).start()
        out_copy(0, m).start()

    for tick in range(half + LAG):
        if tick < half:
            guard(tick, core, functools.partial(arrive, tick))
        if tick >= LAG:
            guard(tick - LAG, core, functools.partial(finish, tick - LAG))

    for m in range(half):

        def receive(m=m):
            share_copy(m).wait_recv()
            out_copy(1, m).start()

        guard(m, 1 - core, receive)

    def angle(r, carry):
        rows = pl.ds(r * ROWS, ROWS)
        inner = power = level = None
        for which in range(2):
            place = core if which == 0 else 1 - core
            sums = [jnp.zeros((ROWS, columns), F32)] * 3
            for m in range(half):
                spot = place * half + m
                valid = spot < ms
                look = jnp.minimum(spot, ms - 1)
                mine = result[which, m, rows, :]
                sight = seen[look, rows, :].astype(F32)
                if half + m >= ms:
                    mine = jnp.where(valid, mine, 0.0)
                    sight = jnp.where(valid, sight, 0.0)
                sums = [
                    sums[0] + mine * sight,
                    sums[1] + mine * mine,
                    sums[2] + sight * sight,
                ]
            inner = sums[0] if inner is None else inner + sums[0]
            power = sums[1] if power is None else power + sums[1]
            level = sums[2] if level is None else level + sums[2]
        norm = jnp.maximum(jnp.sqrt(power) * jnp.sqrt(level), 1.0)
        angle_buf[rows, :] = jnp.clip(inner / norm, -1.0, 1.0)
        return carry

    def blank(which, place):
        for m in range(half):
            if half + m >= ms:

                @pl.when(place * half + m >= ms)
                def _():
                    result[which, m] = jnp.zeros((lines, columns), F32)

    blank(0, core)
    blank(1, 1 - core)
    lax.fori_loop(0, lines // ROWS, angle, 0)
    cos_copy = pltpu.make_async_copy(angle_buf, cosine, arg_sem.at[3])
    cos_copy.start()

    for g in range(groups):
        give_copy(g).wait_send()
    for m in range(half):

        def drain(m=m):
            for copy in code_copies(m):
                copy.wait_send()

            @pl.when(has_ahead)
            def _():
                for copy in pass_copies(m):
                    copy.wait_send()

            share_copy(m).wait_send()
            out_copy(0, m).wait()

        guard(m, core, drain)
        guard(m, 1 - core, lambda m=m: out_copy(1, m).wait())
    cos_copy.wait()


def arccos(x):
    size = jnp.abs(x)
    big = size > 0.5
    square = jnp.where(big, 0.5 - 0.5 * size, size * size)
    root = jnp.where(big, jnp.sqrt(square), size)
    poly = 4.2163199048e-2
    for term in (2.4181311049e-2, 4.5470025998e-2, 7.4953002686e-2, 1.6666752422e-1):
        poly = poly * square + term
    arc = root + root * square * poly
    angle = jnp.where(big, 2.0 * arc, 0.5 * math.pi - arc)
    return jnp.where(x < 0.0, math.pi - angle, angle)


def finish_kernel(synthetic, cosine, synthetic_out, angles_out, angle_buf, sem):
    copy = pltpu.make_async_copy(synthetic, synthetic_out, sem.at[0])
    copy.start()
    angle_buf[...] = arccos(cosine[...])
    last = pltpu.make_async_copy(angle_buf, angles_out, sem.at[1])
    last.start()
    copy.wait()
    last.wait()


def on_device(
    cube,
    observed,
    along_kernels,
    along_offsets,
    across_kernels,
    across_offsets,
    resp_start,
    resp_values,
):
    bands, lines, columns = cube.shape
    ms = observed.shape[0]
    cores = lax.axis_size("band")
    line_size = lax.axis_size("line")
    assert cores == 2 and line_size % 2 == 0 and lines == BLK and bands <= 128
    half = -(-ms // cores)
    groups = lines // ROWS
    sizes = (bands, lines, columns, ms, half, line_size)
    hbm = pl.BlockSpec(memory_space=pltpu.HBM)
    dma = pltpu.SemaphoreType.DMA
    synthetic, cosine = pl.pallas_call(
        functools.partial(kernel, sizes),
        out_shape=(
            pltpu.VMEM((ms, lines, columns), F32),
            pltpu.VMEM((lines, columns), F32),
        ),
        in_specs=[hbm] * 8,
        out_specs=(
            pl.BlockSpec(memory_space=pltpu.VMEM),
            pl.BlockSpec(memory_space=pltpu.VMEM),
        ),
        scratch_shapes=[
            pltpu.VMEM((2 * half * ROWS, bands * ROWS), BF16),
            pltpu.VMEM((groups, bands, ROWS, columns), BF16),
            pltpu.VMEM((ms, lines, columns), BF16),
            pltpu.VMEM((3, BLK, BLK), BF16),
            pltpu.VMEM((3, BLK, BLK), BF16),
            pltpu.VMEM((3, BLK, 2 * BLK), BF16),
            pltpu.VMEM((2 * columns, columns), BF16),
            pltpu.VMEM((groups, half, ROWS, columns), F32),
            pltpu.VMEM((groups, half, ROWS, columns), F32),
            pltpu.VMEM((groups, half, ROWS, columns), F32),
            pltpu.VMEM((half, lines, columns), F32),
            pltpu.VMEM((half, lines, columns), jnp.int16),
            pltpu.VMEM((half, 1, columns), F32),
            pltpu.VMEM((half, lines, columns), jnp.int16),
            pltpu.VMEM((half, 1, columns), F32),
            pltpu.VMEM((half, lines, columns), jnp.int16),
            pltpu.VMEM((half, 1, columns), F32),
            pltpu.VMEM((2, half, lines, columns), F32),
            pltpu.VMEM((lines, columns), F32),
            pltpu.VMEM(resp_values.shape, BF16),
            pltpu.SMEM(along_offsets.shape, jnp.int32),
            pltpu.SMEM(across_offsets.shape, jnp.int32),
            pltpu.SMEM(resp_start.shape, jnp.int32),
            dma((groups,)),
            dma((8,)),
            dma((groups,)),
            dma((groups,)),
        ]
        + [dma((half,))] * 10
        + [dma((2, half))],
        compiler_params=pltpu.CompilerParams(
            collective_id=0, has_side_effects=True, vmem_limit_bytes=48_000_000
        ),
    )(
        *(
            pltpu.with_memory_space_constraint(value, pltpu.HBM)
            for value in (
                cube,
                observed,
                along_kernels,
                across_kernels,
                resp_values,
                along_offsets,
                across_offsets,
                resp_start,
            )
        )
    )
    return pl.pallas_call(
        finish_kernel,
        out_shape=(
            jax.ShapeDtypeStruct((ms, lines, columns), F32),
            jax.ShapeDtypeStruct((lines, columns), F32),
        ),
        in_specs=[pl.BlockSpec(memory_space=pltpu.VMEM)] * 2,
        out_specs=(hbm, hbm),
        scratch_shapes=[pltpu.VMEM((lines, columns), F32), dma((2,))],
        compiler_params=pltpu.CompilerParams(vmem_limit_bytes=8_000_000),
    )(
        pltpu.with_memory_space_constraint(synthetic, pltpu.VMEM),
        pltpu.with_memory_space_constraint(cosine, pltpu.VMEM),
    )


def solution(mesh):
    placed = (
        P("band", ("slab", "line"), None),
        P(None, ("slab", "line"), None),
        P(),
        P(),
        P(),
        P(),
        P(),
        P(),
    )
    return jax.shard_map(
        on_device,
        mesh=mesh,
        in_specs=placed,
        out_specs=(P(None, ("slab", "line"), None), P(("slab", "line"), None)),
        check_vma=False,
    )
```

```python
import functools
import math

import jax
import jax.numpy as jnp
from jax import lax
from jax.experimental import pallas as pl
from jax.experimental.pallas import tpu as pltpu
from jax.sharding import PartitionSpec as P

BLK = 128
SPB = 10
ROWS = 16
EARLY_CHUNKS = 2
CODE_LAG = 4
PIECES = 2
MESH = pl.DeviceIdType.MESH
F32 = jnp.float32
BF16 = jnp.bfloat16
I16 = jnp.int16
PEAK = 32767.0


def halves(value):
    high = value.astype(BF16)
    low = (value - high.astype(F32)).astype(BF16)
    return high, low


def coded_of(value, axes):
    peak = jnp.max(jnp.abs(value), axis=axes, keepdims=True)
    inverse = jnp.where(peak > 0.0, PEAK / jnp.maximum(peak, 1e-30), 0.0)
    code = jnp.round(value * inverse).astype(jnp.int32).astype(I16)
    return code, peak * (1.0 / PEAK)


def value_of(code, scale):
    return code.astype(jnp.int32).astype(F32) * scale


def picked(kernels, offsets, shift):
    total = None
    for k in range(3):
        term = jnp.where(offsets[k] == shift, kernels[k].astype(F32), 0.0)
        total = term if total is None else total + term
    return total


def iota(shape, dim):
    return lax.broadcasted_iota(jnp.int32, shape, dim)


def kernel(
    sizes,
    cube,
    observed,
    along_hbm,
    across_hbm,
    values_hbm,
    along_off_hbm,
    across_off_hbm,
    start_hbm,
    synthetic,
    seen,
    sums,
    folder,
    field,
    along,
    across,
    taps,
    partner_taps,
    mixer,
    given,
    own,
    got,
    coded,
    scale,
    near,
    near_scale,
    far,
    far_scale,
    side,
    side_scale,
    stack,
    base,
    made,
    made_scale,
    came,
    came_scale,
    values,
    along_off,
    across_off,
    start,
    cube_sem,
    arg_sem,
    give_sem,
    near_sem,
    far_sem,
    side_sem,
    came_sem,
    share_sem,
):
    bands, lines, columns, ms, half, direct, line_size = sizes
    groups = lines // ROWS
    relayed = half - direct
    part_lines = lines // PIECES
    core = lax.axis_index("band")
    index = lax.axis_index("line")
    other = {"band": 1 - core}
    even = index % 2 == 0
    partner = {"line": index + 1 - 2 * (index % 2)}
    step = 2 - 4 * (index % 2)
    ahead, behind = index + step, index - step
    has_ahead = jnp.logical_and(ahead >= 0, ahead < line_size)
    has_behind = jnp.logical_and(behind >= 0, behind < line_size)

    def remote(src, dst, sems, spot, device):
        return pltpu.make_async_remote_copy(
            src_ref=src,
            dst_ref=dst,
            send_sem=sems.at[(0, *spot)],
            recv_sem=sems.at[(1, *spot)],
            device_id=device,
            device_id_type=MESH,
        )

    def cube_copy(g):
        return pltpu.make_async_copy(
            cube.at[:, pl.ds(g * ROWS, ROWS), :], field.at[g], cube_sem.at[g]
        )

    def give_copy(g):
        return remote(given.at[g], got.at[g], give_sem, (g,), other)

    def near_copies(g):
        return (
            remote(coded.at[g, pl.ds(0, direct)], near.at[g], near_sem, (0, g), partner),
            remote(scale.at[g], near_scale.at[g], near_sem, (1, g), partner),
        )

    def far_copies(g):
        device = {"line": ahead}
        return (
            remote(near.at[g], far.at[g], far_sem, (0, g), device),
            remote(near_scale.at[g], far_scale.at[g], far_sem, (1, g), device),
        )

    def side_copies(g):
        device = {"line": behind}
        return (
            remote(coded.at[g, pl.ds(direct, relayed)], side.at[g], side_sem, (0, g), device),
            remote(scale.at[g], side_scale.at[g], side_sem, (1, g), device),
        )

    def came_copies(r, piece):
        spot = r * PIECES + piece
        return (
            remote(made.at[r, piece], came.at[r, piece], came_sem, (0, spot), partner),
            remote(made_scale.at[r, piece], came_scale.at[r, piece], came_sem, (1, spot), partner),
        )

    def share_copy(place, k, piece):
        ref = synthetic.at[place * half + k, pl.ds(piece * part_lines, part_lines)]
        return remote(ref, ref, share_sem, (k * PIECES + piece,), other)

    def guard(k, place, body):
        if half + k < ms:
            body()
        else:
            pl.when(place * half + k < ms)(body)

    along_copy = pltpu.make_async_copy(along_hbm, along, arg_sem.at[0])
    across_copy = pltpu.make_async_copy(across_hbm, across, arg_sem.at[1])
    seen_copy = pltpu.make_async_copy(observed, seen, arg_sem.at[2])
    early = [
        pltpu.make_async_copy(values_hbm, values, arg_sem.at[3]),
        pltpu.make_async_copy(start_hbm, start, arg_sem.at[4]),
        pltpu.make_async_copy(along_off_hbm, along_off, arg_sem.at[5]),
        pltpu.make_async_copy(across_off_hbm, across_off, arg_sem.at[6]),
    ]
    for copy in early:
        copy.start()
    for g in range(EARLY_CHUNKS):
        cube_copy(g).start()

    barrier = pltpu.get_barrier_semaphore()
    pl.semaphore_signal(barrier, inc=1, device_id=other, device_id_type=MESH)
    pl.semaphore_signal(barrier, inc=1, device_id=partner, device_id_type=MESH)

    @pl.when(has_ahead)
    def _():
        pl.semaphore_signal(barrier, inc=1, device_id={"line": ahead}, device_id_type=MESH)

    @pl.when(has_behind)
    def _():
        pl.semaphore_signal(barrier, inc=1, device_id={"line": behind}, device_id_type=MESH)

    for copy in early:
        copy.wait()
    for g in range(EARLY_CHUNKS, groups):
        cube_copy(g).start()
    along_copy.start()
    across_copy.start()
    seen_copy.start()

    lane = core * bands + iota((ms, 128), 1)
    row = iota((ms, 128), 0)
    first = jnp.zeros((ms, 128), jnp.int32)
    for m in range(ms):
        first = jnp.where(row == m, start[m], first)
    slot = lane - SPB * first
    weights = values[...].astype(F32)
    response = jnp.zeros((ms, 128), F32)
    for j in range(2 * SPB):
        response = jnp.where(slot == j, weights[:, j : j + 1], response)
    tall = 2 * half * ROWS
    picks = iota((tall, ms), 0) // ROWS
    owner = jnp.where(picks < half, (1 - core) * half + picks, core * half + picks - half)
    choose = (owner == iota((tall, ms), 1)).astype(BF16)
    per_row = jnp.dot(choose, response.astype(BF16), preferred_element_type=F32).astype(BF16)
    wide = bands * ROWS
    spread = (iota((128, wide), 1) // ROWS == iota((128, wide), 0)).astype(BF16)
    spread_rows = jnp.dot(per_row, spread, preferred_element_type=F32)
    same = iota((tall, wide), 0) % ROWS == iota((tall, wide), 1) % ROWS
    folder[...] = jnp.where(same, spread_rows, 0.0).astype(BF16)

    peers = 2 + has_ahead.astype(jnp.int32) + has_behind.astype(jnp.int32)
    pl.semaphore_wait(barrier, peers)

    def place(k, block, g, value):
        high, low = halves(value)
        stack[k, pl.ds(2 * block * lines + g * ROWS, ROWS), :] = high
        stack[k, pl.ds((2 * block + 1) * lines + g * ROWS, ROWS), :] = low

    def fold(g):
        cube_copy(g).wait()
        block = field[g].reshape(wide, columns)
        part = jnp.dot(folder[...], block, preferred_element_type=F32)
        part = part.reshape(2 * half, ROWS, columns)
        given[g] = part[:half]
        own[g] = part[half:]
        give_copy(g).start()

    def encode(g):
        give_copy(g).wait_recv()
        value = own[g] + got[g]
        code, unit = coded_of(value, (0, 1))
        coded[g] = code
        scale[g] = unit[0]
        for copy in near_copies(g):
            copy.start()

        @pl.when(has_behind)
        def _():
            for copy in side_copies(g):
                copy.start()

        for k in range(half):
            place(k, 0, g, value[k])

    for g in range(groups):
        fold(g)
        if g >= CODE_LAG:
            encode(g - CODE_LAG)
    for g in range(groups - CODE_LAG, groups):
        encode(g)

    along_copy.wait()
    across_copy.wait()
    before, after = (picked(along, along_off, -1), picked(along, along_off, 1))
    middle = picked(along, along_off, 0)
    near_tap = jnp.where(even, after, before).astype(BF16)
    far_tap = jnp.where(even, before, after).astype(BF16)
    middle = middle.astype(BF16)
    taps[...] = jnp.concatenate([middle, middle, near_tap, near_tap, far_tap, far_tap], axis=1)
    partner_taps[...] = jnp.concatenate([far_tap, far_tap, near_tap, near_tap], axis=1)
    count = columns // BLK
    mixer[...] = jnp.zeros(mixer.shape, BF16)
    for shift in (-1, 0, 1):
        turned = jnp.transpose(picked(across, across_off, shift)).astype(BF16)
        for j in range(count):
            if 0 <= j + shift < count:
                for part in range(2):
                    top = part * columns + (j + shift) * BLK
                    mixer[top : top + BLK, j * BLK : (j + 1) * BLK] = turned

    @pl.when(jnp.logical_not(has_behind))
    def _():
        stack[0:direct, 4 * lines : 6 * lines, :] = jnp.zeros((direct, 2 * lines, columns), BF16)

    @pl.when(jnp.logical_not(has_ahead))
    def _():
        stack[direct:half, 2 * lines : 4 * lines, :] = jnp.zeros((relayed, 2 * lines, columns), BF16)

    def mixed(smooth):
        both = jnp.concatenate(halves(smooth), axis=1)
        return jnp.dot(both, mixer[...], preferred_element_type=F32)

    def take_near(g):
        for copy in near_copies(g):
            copy.wait_recv()

        @pl.when(has_ahead)
        def _():
            for copy in far_copies(g):
                copy.start()

        for k in range(direct):
            place(k, 1, g, value_of(near[g, k], near_scale[g]))

    def take_side(g):
        @pl.when(has_ahead)
        def _():
            for copy in side_copies(g):
                copy.wait_recv()
            for r in range(relayed):
                place(direct + r, 1, g, value_of(side[g, r], side_scale[g]))

    def take_far(g):
        @pl.when(has_behind)
        def _():
            for copy in far_copies(g):
                copy.wait_recv()
            for k in range(direct):
                place(k, 2, g, value_of(far[g, k], far_scale[g]))

    def make(r):
        k = direct + r

        def body():
            smooth = jnp.dot(
                partner_taps[...], stack[k, 0 : 4 * lines, :], preferred_element_type=F32
            )
            full = mixed(smooth)
            for piece in range(PIECES):
                rows = full[piece * part_lines : (piece + 1) * part_lines]
                made[r, piece], made_scale[r, piece] = coded_of(rows, 0)
                for copy in came_copies(r, piece):
                    copy.start()

        guard(k, core, body)

    def begin(r):
        k = direct + r

        def body():
            smooth = jnp.dot(
                taps[:, 0 : 2 * lines], stack[k, 0 : 2 * lines, :], preferred_element_type=F32
            )
            base[r] = mixed(smooth)

        guard(k, core, body)

    def finish_direct(k):
        smooth = jnp.dot(taps[...], stack[k], preferred_element_type=F32)
        synthetic[core * half + k] = mixed(smooth)
        for piece in range(PIECES):
            share_copy(core, k, piece).start()

    def finish_relayed(r, piece):
        k = direct + r

        def body():
            for copy in came_copies(r, piece):
                copy.wait_recv()
            rows = pl.ds(piece * part_lines, part_lines)
            added = value_of(came[r, piece], came_scale[r, piece])
            synthetic[core * half + k, rows, :] = base[r, rows, :] + added
            share_copy(core, k, piece).start()

        guard(k, core, body)

    def tally(places):
        def body(t, carry):
            rows = pl.ds(t * ROWS, ROWS)
            inner, power = sums[0, rows, :], sums[1, rows, :]
            for spot in places:
                mine = synthetic[spot, rows, :]
                inner += mine * seen[spot, rows, :].astype(F32)
                power += mine * mine
            sums[0, rows, :] = inner
            sums[1, rows, :] = power
            return carry

        lax.fori_loop(0, groups, body, 0)

    def measure(t, carry):
        rows = pl.ds(t * ROWS, ROWS)
        level = jnp.zeros((ROWS, columns), F32)
        for m in range(ms):
            sight = seen[m, rows, :].astype(F32)
            level += sight * sight
        sums[0, rows, :] = jnp.zeros((ROWS, columns), F32)
        sums[1, rows, :] = jnp.zeros((ROWS, columns), F32)
        sums[2, rows, :] = level
        return carry

    take_near(0)
    take_side(0)
    take_near(1)
    take_side(1)
    take_side(2)
    seen_copy.wait()
    lax.fori_loop(0, groups, measure, 0)
    take_near(2)
    take_side(3)
    begin(0)
    take_near(3)
    take_side(4)
    take_side(5)
    for r in range(1, relayed):
        begin(r)
    take_near(4)
    take_side(6)
    take_side(7)
    make(0)
    take_near(5)
    make(1)
    take_near(6)
    for r in range(2, relayed):
        make(r)
    take_near(7)
    for g in range(groups):
        take_far(g)
    for k in range(direct):
        finish_direct(k)
    tally([core * half + k for k in range(direct)])
    for piece in range(PIECES):
        finish_relayed(0, piece)
    for k in range(direct):
        for piece in range(PIECES):
            share_copy(1 - core, k, piece).wait_recv()
    tally([(1 - core) * half + k for k in range(direct)])
    for r in range(1, relayed):
        for piece in range(PIECES):
            finish_relayed(r, piece)

    for g in range(groups):
        give_copy(g).wait_send()
        for copy in near_copies(g):
            copy.wait_send()

        @pl.when(has_ahead)
        def _():
            for copy in far_copies(g):
                copy.wait_send()

        @pl.when(has_behind)
        def _():
            for copy in side_copies(g):
                copy.wait_send()

    for k in range(half):

        def drain(k=k):
            for piece in range(PIECES):
                share_copy(core, k, piece).wait_send()
                if k >= direct:
                    for copy in came_copies(k - direct, piece):
                        copy.wait_send()

        def receive(k=k):
            for piece in range(PIECES):
                share_copy(1 - core, k, piece).wait_recv()

        guard(k, core, drain)
        if k >= direct:
            guard(k, 1 - core, receive)


def arccos(x):
    size = jnp.abs(x)
    big = size > 0.5
    square = jnp.where(big, 0.5 - 0.5 * size, size * size)
    root = jnp.where(big, jnp.sqrt(square), size)
    poly = 4.2163199048e-2
    for term in (2.4181311049e-2, 4.5470025998e-2, 7.4953002686e-2, 1.6666752422e-1):
        poly = poly * square + term
    arc = root + root * square * poly
    angle = jnp.where(big, 2.0 * arc, 0.5 * math.pi - arc)
    return jnp.where(x < 0.0, math.pi - angle, angle)


def finish_kernel(places, synthetic, seen, sums, synthetic_out, angles_out, angles, sem):
    copy = pltpu.make_async_copy(synthetic, synthetic_out, sem.at[0])
    copy.start()

    def angle(t, carry):
        rows = pl.ds(t * ROWS, ROWS)
        inner, power, level = (sums[n, rows, :] for n in range(3))
        for spot in places:
            mine = synthetic[spot, rows, :]
            inner += mine * seen[spot, rows, :].astype(F32)
            power += mine * mine
        norm = jnp.maximum(jnp.sqrt(power) * jnp.sqrt(level), 1.0)
        angles[rows, :] = arccos(jnp.clip(inner / norm, -1.0, 1.0))
        return carry

    lax.fori_loop(0, angles.shape[0] // ROWS, angle, 0)
    last = pltpu.make_async_copy(angles, angles_out, sem.at[1])
    last.start()
    copy.wait()
    last.wait()


def on_device(
    cube,
    observed,
    along_kernels,
    along_offsets,
    across_kernels,
    across_offsets,
    resp_start,
    resp_values,
):
    bands, lines, columns = cube.shape
    ms = observed.shape[0]
    cores = lax.axis_size("band")
    line_size = lax.axis_size("line")
    assert cores == 2 and line_size % 2 == 0 and lines == BLK and bands <= 128
    half = -(-ms // cores)
    direct = (half + 1) // 2
    relayed = half - direct
    groups = lines // ROWS
    part_lines = lines // PIECES
    sizes = (bands, lines, columns, ms, half, direct, line_size)
    hbm = pl.BlockSpec(memory_space=pltpu.HBM)
    vmem = pl.BlockSpec(memory_space=pltpu.VMEM)
    dma = pltpu.SemaphoreType.DMA
    results = pl.pallas_call(
        functools.partial(kernel, sizes),
        out_shape=(
            pltpu.VMEM((ms, lines, columns), F32),
            pltpu.VMEM((ms, lines, columns), BF16),
            pltpu.VMEM((3, lines, columns), F32),
        ),
        in_specs=[hbm] * 8,
        out_specs=(vmem,) * 3,
        scratch_shapes=[
            pltpu.VMEM((2 * half * ROWS, bands * ROWS), BF16),
            pltpu.VMEM((groups, bands, ROWS, columns), BF16),
            pltpu.VMEM((3, BLK, BLK), BF16),
            pltpu.VMEM((3, BLK, BLK), BF16),
            pltpu.VMEM((BLK, 6 * BLK), BF16),
            pltpu.VMEM((BLK, 4 * BLK), BF16),
            pltpu.VMEM((2 * columns, columns), BF16),
            pltpu.VMEM((groups, half, ROWS, columns), F32),
            pltpu.VMEM((groups, half, ROWS, columns), F32),
            pltpu.VMEM((groups, half, ROWS, columns), F32),
            pltpu.VMEM((groups, half, ROWS, columns), I16),
            pltpu.VMEM((groups, 1, columns), F32),
            pltpu.VMEM((groups, direct, ROWS, columns), I16),
            pltpu.VMEM((groups, 1, columns), F32),
            pltpu.VMEM((groups, direct, ROWS, columns), I16),
            pltpu.VMEM((groups, 1, columns), F32),
            pltpu.VMEM((groups, relayed, ROWS, columns), I16),
            pltpu.VMEM((groups, 1, columns), F32),
            pltpu.VMEM((half, 6 * lines, columns), BF16),
            pltpu.VMEM((relayed, lines, columns), F32),
            pltpu.VMEM((relayed, PIECES, part_lines, columns), I16),
            pltpu.VMEM((relayed, PIECES, 1, columns), F32),
            pltpu.VMEM((relayed, PIECES, part_lines, columns), I16),
            pltpu.VMEM((relayed, PIECES, 1, columns), F32),
            pltpu.VMEM(resp_values.shape, BF16),
            pltpu.SMEM(along_offsets.shape, jnp.int32),
            pltpu.SMEM(across_offsets.shape, jnp.int32),
            pltpu.SMEM(resp_start.shape, jnp.int32),
            dma((groups,)),
            dma((7,)),
            dma((2, groups)),
            dma((2, 2, groups)),
            dma((2, 2, groups)),
            dma((2, 2, groups)),
            dma((2, 2, relayed * PIECES)),
            dma((2, half * PIECES)),
        ],
        compiler_params=pltpu.CompilerParams(
            collective_id=0, has_side_effects=True, vmem_limit_bytes=48_000_000
        ),
    )(
        *(
            pltpu.with_memory_space_constraint(value, pltpu.HBM)
            for value in (
                cube,
                observed,
                along_kernels,
                across_kernels,
                resp_values,
                along_offsets,
                across_offsets,
                resp_start,
            )
        )
    )
    places = [m for m in range(ms) if m % half >= direct]
    return pl.pallas_call(
        functools.partial(finish_kernel, places),
        out_shape=(
            jax.ShapeDtypeStruct((ms, lines, columns), F32),
            jax.ShapeDtypeStruct((lines, columns), F32),
        ),
        in_specs=[vmem] * 3,
        out_specs=(hbm, hbm),
        scratch_shapes=[pltpu.VMEM((lines, columns), F32), dma((2,))],
        compiler_params=pltpu.CompilerParams(vmem_limit_bytes=8_000_000),
    )(*(pltpu.with_memory_space_constraint(value, pltpu.VMEM) for value in results))


def solution(mesh):
    placed = (
        P("band", ("slab", "line"), None),
        P(None, ("slab", "line"), None),
        P(),
        P(),
        P(),
        P(),
        P(),
        P(),
    )
    return jax.shard_map(
        on_device,
        mesh=mesh,
        in_specs=placed,
        out_specs=(P(None, ("slab", "line"), None), P(("slab", "line"), None)),
        check_vma=False,
    )
```

```python
import functools
import math

import jax
import jax.numpy as jnp
from jax import lax
from jax.experimental import pallas as pl
from jax.experimental.pallas import tpu as pltpu
from jax.sharding import PartitionSpec as P

BLK = 128
SPB = 10
ROWS = 16
EARLY_GROUPS = 2
CHUNKS = (1, 1, 2, 2, 2)
ORDER = "f0 f1 f2 e0 e1 f3 e2 f4 e3 e4"
PIECES = 2
MESH = pl.DeviceIdType.MESH
F32 = jnp.float32
BF16 = jnp.bfloat16
I16 = jnp.int16
PEAK = 32767.0


def halves(value):
    high = value.astype(BF16)
    low = (value - high.astype(F32)).astype(BF16)
    return high, low


def coded_of(value, axes):
    peak = jnp.max(jnp.abs(value), axis=axes, keepdims=True)
    inverse = jnp.where(peak > 0.0, PEAK / jnp.maximum(peak, 1e-30), 0.0)
    code = jnp.round(value * inverse).astype(jnp.int32).astype(I16)
    return code, peak * (1.0 / PEAK)


def value_of(code, scale):
    return code.astype(jnp.int32).astype(F32) * scale


def picked(kernels, offsets, shift):
    total = None
    for k in range(3):
        term = jnp.where(offsets[k] == shift, kernels[k].astype(F32), 0.0)
        total = term if total is None else total + term
    return total


def iota(shape, dim):
    return lax.broadcasted_iota(jnp.int32, shape, dim)


def kernel(
    sizes,
    cube,
    observed,
    along_hbm,
    across_hbm,
    values_hbm,
    along_off_hbm,
    across_off_hbm,
    start_hbm,
    synthetic,
    seen,
    sums,
    folder,
    field,
    along,
    across,
    taps,
    partner_taps,
    mixer,
    given,
    own,
    got,
    coded,
    scale,
    near,
    near_scale,
    far,
    far_scale,
    side,
    side_scale,
    stack,
    base,
    early_sum,
    made,
    made_scale,
    came,
    came_scale,
    values,
    along_off,
    across_off,
    start,
    cube_sem,
    arg_sem,
    give_sem,
    near_sem,
    far_sem,
    side_sem,
    came_sem,
    share_sem,
):
    bands, lines, columns, ms, half, direct, line_size = sizes
    groups = lines // ROWS
    relayed = half - direct
    part_lines = lines // PIECES
    core = lax.axis_index("band")
    index = lax.axis_index("line")
    mine, theirs = 1 - core, core
    other = {"band": 1 - core}
    even = index % 2 == 0
    partner = {"line": index + 1 - 2 * (index % 2)}
    step = 2 - 4 * (index % 2)
    ahead, behind = index + step, index - step
    has_ahead = jnp.logical_and(ahead >= 0, ahead < line_size)
    has_behind = jnp.logical_and(behind >= 0, behind < line_size)

    def remote(src, dst, sems, spot, device):
        return pltpu.make_async_remote_copy(
            src_ref=src,
            dst_ref=dst,
            send_sem=sems.at[(0, *spot)],
            recv_sem=sems.at[(1, *spot)],
            device_id=device,
            device_id_type=MESH,
        )

    def cube_copy(g):
        return pltpu.make_async_copy(
            cube.at[:, pl.ds(g * ROWS, ROWS), :], field.at[g], cube_sem.at[g]
        )

    chunks = []
    for size in CHUNKS:
        begin_at = chunks[-1][0] + chunks[-1][1] if chunks else 0
        chunks.append((begin_at, size))

    def give_copy(c):
        part = pl.ds(*chunks[c])
        return remote(given.at[part], got.at[part], give_sem, (c,), other)

    def near_copies(g):
        return (
            remote(coded.at[g, pl.ds(0, direct)], near.at[g], near_sem, (0, g), partner),
            remote(scale.at[g], near_scale.at[g], near_sem, (1, g), partner),
        )

    def far_copies(g):
        device = {"line": ahead}
        return (
            remote(near.at[g], far.at[g], far_sem, (0, g), device),
            remote(near_scale.at[g], far_scale.at[g], far_sem, (1, g), device),
        )

    def side_copies(g):
        device = {"line": behind}
        return (
            remote(coded.at[g, pl.ds(direct, relayed)], side.at[g], side_sem, (0, g), device),
            remote(scale.at[g], side_scale.at[g], side_sem, (1, g), device),
        )

    def came_copies(r, piece):
        spot = r * PIECES + piece
        return (
            remote(made.at[r, piece], came.at[r, piece], came_sem, (0, spot), partner),
            remote(made_scale.at[r, piece], came_scale.at[r, piece], came_sem, (1, spot), partner),
        )

    def share_copy(place, k, piece):
        ref = synthetic.at[place * half + k, pl.ds(piece * part_lines, part_lines)]
        return remote(ref, ref, share_sem, (k * PIECES + piece,), other)

    def guard(k, place, body):
        if half + k < ms:
            body()
        else:
            pl.when(place * half + k < ms)(body)

    along_copy = pltpu.make_async_copy(along_hbm, along, arg_sem.at[0])
    across_copy = pltpu.make_async_copy(across_hbm, across, arg_sem.at[1])
    seen_copy = pltpu.make_async_copy(observed, seen, arg_sem.at[2])
    early = [
        pltpu.make_async_copy(values_hbm, values, arg_sem.at[3]),
        pltpu.make_async_copy(start_hbm, start, arg_sem.at[4]),
        pltpu.make_async_copy(along_off_hbm, along_off, arg_sem.at[5]),
        pltpu.make_async_copy(across_off_hbm, across_off, arg_sem.at[6]),
    ]
    for copy in early:
        copy.start()
    for g in range(EARLY_GROUPS):
        cube_copy(g).start()

    barrier = pltpu.get_barrier_semaphore()
    pl.semaphore_signal(barrier, inc=1, device_id=other, device_id_type=MESH)
    pl.semaphore_signal(barrier, inc=1, device_id=partner, device_id_type=MESH)

    @pl.when(has_ahead)
    def _():
        pl.semaphore_signal(barrier, inc=1, device_id={"line": ahead}, device_id_type=MESH)

    @pl.when(has_behind)
    def _():
        pl.semaphore_signal(barrier, inc=1, device_id={"line": behind}, device_id_type=MESH)

    for copy in early:
        copy.wait()
    for g in range(EARLY_GROUPS, groups):
        cube_copy(g).start()
    along_copy.start()
    across_copy.start()
    seen_copy.start()

    lane = core * bands + iota((ms, 128), 1)
    row = iota((ms, 128), 0)
    first = jnp.zeros((ms, 128), jnp.int32)
    for m in range(ms):
        first = jnp.where(row == m, start[m], first)
    slot = lane - SPB * first
    weights = values[...].astype(F32)
    response = jnp.zeros((ms, 128), F32)
    for j in range(2 * SPB):
        response = jnp.where(slot == j, weights[:, j : j + 1], response)
    tall = 2 * half * ROWS
    picks = iota((tall, ms), 0) // ROWS
    owner = jnp.where(picks < half, theirs * half + picks, mine * half + picks - half)
    choose = (owner == iota((tall, ms), 1)).astype(BF16)
    per_row = jnp.dot(choose, response.astype(BF16), preferred_element_type=F32).astype(BF16)
    wide = bands * ROWS
    spread = (iota((128, wide), 1) // ROWS == iota((128, wide), 0)).astype(BF16)
    spread_rows = jnp.dot(per_row, spread, preferred_element_type=F32)
    same = iota((tall, wide), 0) % ROWS == iota((tall, wide), 1) % ROWS
    folder[...] = jnp.where(same, spread_rows, 0.0).astype(BF16)

    peers = 2 + has_ahead.astype(jnp.int32) + has_behind.astype(jnp.int32)

    def place(k, block, g, value):
        high, low = halves(value)
        stack[k, pl.ds(2 * block * lines + g * ROWS, ROWS), :] = high
        stack[k, pl.ds((2 * block + 1) * lines + g * ROWS, ROWS), :] = low

    def fold(c):
        first_group, size = chunks[c]
        for g in range(first_group, first_group + size):
            cube_copy(g).wait()
        for g in range(first_group, first_group + size):
            block = field[g].reshape(wide, columns)
            part = jnp.dot(folder[...], block, preferred_element_type=F32)
            part = part.reshape(2 * half, ROWS, columns)
            given[g] = part[:half]
            own[g] = part[half:]

    def encode(c):
        first_group, size = chunks[c]
        give_copy(c).wait_recv()
        for g in range(first_group, first_group + size):
            code, unit = coded_of(own[g] + got[g], (0, 1))
            coded[g] = code
            scale[g] = unit[0]
        for g in range(first_group, first_group + size):
            for copy in near_copies(g):
                copy.start()

        @pl.when(has_behind)
        def _():
            for g in range(first_group, first_group + size):
                for copy in side_copies(g):
                    copy.start()

        for g in range(first_group, first_group + size):
            value = own[g] + got[g]
            for k in range(half):
                place(k, 0, g, value[k])

    for step in ORDER.split():
        c = int(step[1:])
        if step[0] == "f":
            fold(c)
            if c == 0:
                pl.semaphore_wait(barrier, peers)
            give_copy(c).start()
        else:
            encode(c)

    along_copy.wait()
    across_copy.wait()
    before, after = (picked(along, along_off, -1), picked(along, along_off, 1))
    middle = picked(along, along_off, 0)
    near_tap = jnp.where(even, after, before).astype(BF16)
    far_tap = jnp.where(even, before, after).astype(BF16)
    middle = middle.astype(BF16)
    taps[...] = jnp.concatenate([middle, middle, near_tap, near_tap, far_tap, far_tap], axis=1)
    partner_taps[...] = jnp.concatenate([far_tap, far_tap, near_tap, near_tap], axis=1)
    count = columns // BLK
    mixer[...] = jnp.zeros(mixer.shape, BF16)
    for shift in (-1, 0, 1):
        turned = jnp.transpose(picked(across, across_off, shift)).astype(BF16)
        for j in range(count):
            if 0 <= j + shift < count:
                for part in range(2):
                    top = part * columns + (j + shift) * BLK
                    mixer[top : top + BLK, j * BLK : (j + 1) * BLK] = turned

    @pl.when(jnp.logical_not(has_behind))
    def _():
        stack[0:direct, 4 * lines : 6 * lines, :] = jnp.zeros((direct, 2 * lines, columns), BF16)

    @pl.when(jnp.logical_not(has_ahead))
    def _():
        stack[direct:half, 2 * lines : 4 * lines, :] = jnp.zeros((relayed, 2 * lines, columns), BF16)

    def mixed(smooth):
        both = jnp.concatenate(halves(smooth), axis=1)
        return jnp.dot(both, mixer[...], preferred_element_type=F32)

    def take_near(g):
        for copy in near_copies(g):
            copy.wait_recv()

        @pl.when(has_ahead)
        def _():
            for copy in far_copies(g):
                copy.start()

        for k in range(direct):
            place(k, 1, g, value_of(near[g, k], near_scale[g]))

    def take_side(g):
        @pl.when(has_ahead)
        def _():
            for copy in side_copies(g):
                copy.wait_recv()
            for r in range(relayed):
                place(direct + r, 1, g, value_of(side[g, r], side_scale[g]))

    def take_far(g):
        @pl.when(has_behind)
        def _():
            for copy in far_copies(g):
                copy.wait_recv()
            for k in range(direct):
                place(k, 2, g, value_of(far[g, k], far_scale[g]))

    def make(r):
        k = direct + r

        def body():
            smooth = jnp.dot(
                partner_taps[...], stack[k, 0 : 4 * lines, :], preferred_element_type=F32
            )
            full = mixed(smooth)
            for piece in range(PIECES):
                rows = full[piece * part_lines : (piece + 1) * part_lines]
                made[r, piece], made_scale[r, piece] = coded_of(rows, 0)
                for copy in came_copies(r, piece):
                    copy.start()

        guard(k, mine, body)

    def begin(r):
        k = direct + r

        def body():
            smooth = jnp.dot(
                taps[:, 0 : 2 * lines], stack[k, 0 : 2 * lines, :], preferred_element_type=F32
            )
            base[r] = mixed(smooth)

        guard(k, mine, body)

    def begin_direct(k):
        smooth = jnp.dot(
            taps[:, 0 : 4 * lines], stack[k, 0 : 4 * lines, :], preferred_element_type=F32
        )
        early_sum[k] = mixed(smooth)

    def finish_direct(k):
        smooth = jnp.dot(
            taps[:, 4 * lines :], stack[k, 4 * lines :, :], preferred_element_type=F32
        )
        synthetic[mine * half + k] = early_sum[k] + mixed(smooth)
        for piece in range(PIECES):
            share_copy(mine, k, piece).start()

    def finish_relayed(r, piece):
        k = direct + r

        def body():
            for copy in came_copies(r, piece):
                copy.wait_recv()
            rows = pl.ds(piece * part_lines, part_lines)
            added = value_of(came[r, piece], came_scale[r, piece])
            synthetic[mine * half + k, rows, :] = base[r, rows, :] + added
            share_copy(mine, k, piece).start()

        guard(k, mine, body)

    def tally(places):
        def body(t, carry):
            rows = pl.ds(t * ROWS, ROWS)
            inner, power = sums[0, rows, :], sums[1, rows, :]
            for spot in places:
                mine = synthetic[spot, rows, :]
                inner += mine * seen[spot, rows, :].astype(F32)
                power += mine * mine
            sums[0, rows, :] = inner
            sums[1, rows, :] = power
            return carry

        lax.fori_loop(0, groups, body, 0)

    def measure(t, carry):
        rows = pl.ds(t * ROWS, ROWS)
        level = jnp.zeros((ROWS, columns), F32)
        for m in range(ms):
            sight = seen[m, rows, :].astype(F32)
            level += sight * sight
        sums[0, rows, :] = jnp.zeros((ROWS, columns), F32)
        sums[1, rows, :] = jnp.zeros((ROWS, columns), F32)
        sums[2, rows, :] = level
        return carry

    take_near(0)
    take_side(0)
    take_near(1)
    take_side(1)
    seen_copy.wait()
    lax.fori_loop(0, groups, measure, 0)
    take_side(2)
    take_near(2)
    take_side(3)
    begin(0)
    take_near(3)
    take_side(4)
    take_side(5)
    for r in range(1, relayed):
        begin(r)
    take_near(4)
    take_side(6)
    take_near(5)
    take_side(7)
    make(0)
    take_near(6)
    make(1)
    take_near(7)
    for r in range(2, relayed):
        make(r)
    for g in range(groups - 3):
        take_far(g)
    for k in range(direct):
        begin_direct(k)
    for piece in range(PIECES):
        finish_relayed(0, piece)
    for g in range(groups - 3, groups):
        take_far(g)
    for k in range(direct):
        finish_direct(k)
    for r in range(1, relayed):
        for piece in range(PIECES):
            finish_relayed(r, piece)
    tally([mine * half + k for k in range(direct)])
    for k in range(direct):
        for piece in range(PIECES):
            share_copy(theirs, k, piece).wait_recv()
    tally([theirs * half + k for k in range(direct)])

    for c in range(len(chunks)):
        give_copy(c).wait_send()
    for g in range(groups):
        for copy in near_copies(g):
            copy.wait_send()

        @pl.when(has_ahead)
        def _():
            for copy in far_copies(g):
                copy.wait_send()

        @pl.when(has_behind)
        def _():
            for copy in side_copies(g):
                copy.wait_send()

    for k in range(half):

        def drain(k=k):
            for piece in range(PIECES):
                share_copy(mine, k, piece).wait_send()
                if k >= direct:
                    for copy in came_copies(k - direct, piece):
                        copy.wait_send()

        def receive(k=k):
            for piece in range(PIECES):
                share_copy(theirs, k, piece).wait_recv()

        guard(k, mine, drain)
        if k >= direct:
            guard(k, theirs, receive)


def arccos(x):
    size = jnp.abs(x)
    big = size > 0.5
    square = jnp.where(big, 0.5 - 0.5 * size, size * size)
    root = jnp.where(big, jnp.sqrt(square), size)
    poly = 4.2163199048e-2
    for term in (2.4181311049e-2, 4.5470025998e-2, 7.4953002686e-2, 1.6666752422e-1):
        poly = poly * square + term
    arc = root + root * square * poly
    angle = jnp.where(big, 2.0 * arc, 0.5 * math.pi - arc)
    return jnp.where(x < 0.0, math.pi - angle, angle)


def finish_kernel(places, synthetic, seen, sums, synthetic_out, angles_out, angles, sem):
    copy = pltpu.make_async_copy(synthetic, synthetic_out, sem.at[0])
    copy.start()

    def angle(t, carry):
        rows = pl.ds(t * ROWS, ROWS)
        inner, power, level = (sums[n, rows, :] for n in range(3))
        for spot in places:
            mine = synthetic[spot, rows, :]
            inner += mine * seen[spot, rows, :].astype(F32)
            power += mine * mine
        norm = jnp.maximum(jnp.sqrt(power) * jnp.sqrt(level), 1.0)
        angles[rows, :] = arccos(jnp.clip(inner / norm, -1.0, 1.0))
        return carry

    lax.fori_loop(0, angles.shape[0] // ROWS, angle, 0)
    last = pltpu.make_async_copy(angles, angles_out, sem.at[1])
    last.start()
    copy.wait()
    last.wait()


def on_device(
    cube,
    observed,
    along_kernels,
    along_offsets,
    across_kernels,
    across_offsets,
    resp_start,
    resp_values,
):
    bands, lines, columns = cube.shape
    ms = observed.shape[0]
    cores = lax.axis_size("band")
    line_size = lax.axis_size("line")
    assert cores == 2 and line_size % 2 == 0 and lines == BLK and bands <= 128
    half = -(-ms // cores)
    direct = (half + 1) // 2
    relayed = half - direct
    groups = lines // ROWS
    assert sum(CHUNKS) == groups
    part_lines = lines // PIECES
    sizes = (bands, lines, columns, ms, half, direct, line_size)
    hbm = pl.BlockSpec(memory_space=pltpu.HBM)
    vmem = pl.BlockSpec(memory_space=pltpu.VMEM)
    dma = pltpu.SemaphoreType.DMA
    results = pl.pallas_call(
        functools.partial(kernel, sizes),
        out_shape=(
            pltpu.VMEM((ms, lines, columns), F32),
            pltpu.VMEM((ms, lines, columns), BF16),
            pltpu.VMEM((3, lines, columns), F32),
        ),
        in_specs=[hbm] * 8,
        out_specs=(vmem,) * 3,
        scratch_shapes=[
            pltpu.VMEM((2 * half * ROWS, bands * ROWS), BF16),
            pltpu.VMEM((groups, bands, ROWS, columns), BF16),
            pltpu.VMEM((3, BLK, BLK), BF16),
            pltpu.VMEM((3, BLK, BLK), BF16),
            pltpu.VMEM((BLK, 6 * BLK), BF16),
            pltpu.VMEM((BLK, 4 * BLK), BF16),
            pltpu.VMEM((2 * columns, columns), BF16),
            pltpu.VMEM((groups, half, ROWS, columns), F32),
            pltpu.VMEM((groups, half, ROWS, columns), F32),
            pltpu.VMEM((groups, half, ROWS, columns), F32),
            pltpu.VMEM((groups, half, ROWS, columns), I16),
            pltpu.VMEM((groups, 1, columns), F32),
            pltpu.VMEM((groups, direct, ROWS, columns), I16),
            pltpu.VMEM((groups, 1, columns), F32),
            pltpu.VMEM((groups, direct, ROWS, columns), I16),
            pltpu.VMEM((groups, 1, columns), F32),
            pltpu.VMEM((groups, relayed, ROWS, columns), I16),
            pltpu.VMEM((groups, 1, columns), F32),
            pltpu.VMEM((half, 6 * lines, columns), BF16),
            pltpu.VMEM((relayed, lines, columns), F32),
            pltpu.VMEM((direct, lines, columns), F32),
            pltpu.VMEM((relayed, PIECES, part_lines, columns), I16),
            pltpu.VMEM((relayed, PIECES, 1, columns), F32),
            pltpu.VMEM((relayed, PIECES, part_lines, columns), I16),
            pltpu.VMEM((relayed, PIECES, 1, columns), F32),
            pltpu.VMEM(resp_values.shape, BF16),
            pltpu.SMEM(along_offsets.shape, jnp.int32),
            pltpu.SMEM(across_offsets.shape, jnp.int32),
            pltpu.SMEM(resp_start.shape, jnp.int32),
            dma((groups,)),
            dma((7,)),
            dma((2, len(CHUNKS))),
            dma((2, 2, groups)),
            dma((2, 2, groups)),
            dma((2, 2, groups)),
            dma((2, 2, relayed * PIECES)),
            dma((2, half * PIECES)),
        ],
        compiler_params=pltpu.CompilerParams(
            collective_id=0, has_side_effects=True, vmem_limit_bytes=48_000_000
        ),
    )(
        *(
            pltpu.with_memory_space_constraint(value, pltpu.HBM)
            for value in (
                cube,
                observed,
                along_kernels,
                across_kernels,
                resp_values,
                along_offsets,
                across_offsets,
                resp_start,
            )
        )
    )
    places = [m for m in range(ms) if m % half >= direct]
    return pl.pallas_call(
        functools.partial(finish_kernel, places),
        out_shape=(
            jax.ShapeDtypeStruct((ms, lines, columns), F32),
            jax.ShapeDtypeStruct((lines, columns), F32),
        ),
        in_specs=[vmem] * 3,
        out_specs=(hbm, hbm),
        scratch_shapes=[pltpu.VMEM((lines, columns), F32), dma((2,))],
        compiler_params=pltpu.CompilerParams(vmem_limit_bytes=8_000_000),
    )(*(pltpu.with_memory_space_constraint(value, pltpu.VMEM) for value in results))


def solution(mesh):
    placed = (
        P("band", ("slab", "line"), None),
        P(None, ("slab", "line"), None),
        P(),
        P(),
        P(),
        P(),
        P(),
        P(),
    )
    return jax.shard_map(
        on_device,
        mesh=mesh,
        in_specs=placed,
        out_specs=(P(None, ("slab", "line"), None), P(("slab", "line"), None)),
        check_vma=False,
    )
```

```python
import functools
import math

import jax
import jax.numpy as jnp
from jax import lax
from jax.experimental import pallas as pl
from jax.experimental.pallas import tpu as pltpu
from jax.sharding import PartitionSpec as P

BLK = 128
SPB = 10
ROWS = 16
EARLY_CHUNKS = 2
CHUNKS = (1, 1, 2, 2, 2)
ORDER = "f0 f1 f2 e0 e1 f3 e2 f4 e3 e4"
PARTS = (1, 1, 1)
TEAM = 2
MESH = pl.DeviceIdType.MESH
F32 = jnp.float32
BF16 = jnp.bfloat16
I16 = jnp.int16
PEAK = 32767.0


def halves(value):
    high = value.astype(BF16)
    low = (value - high.astype(F32)).astype(BF16)
    return high, low


def coded_of(value, axes):
    peak = jnp.max(jnp.abs(value), axis=axes, keepdims=True)
    inverse = jnp.where(peak > 0.0, PEAK / jnp.maximum(peak, 1e-30), 0.0)
    code = jnp.round(value * inverse).astype(jnp.int32).astype(I16)
    return code, peak * (1.0 / PEAK)


def value_of(code, scale):
    return code.astype(jnp.int32).astype(F32) * scale


def picked(kernels, offsets, shift):
    total = None
    for k in range(3):
        term = jnp.where(offsets[k] == shift, kernels[k].astype(F32), 0.0)
        total = term if total is None else total + term
    return total


def iota(shape, dim):
    return lax.broadcasted_iota(jnp.int32, shape, dim)


def kernel(
    sizes,
    cube,
    observed,
    along_hbm,
    across_hbm,
    values_hbm,
    along_off_hbm,
    across_off_hbm,
    start_hbm,
    synthetic,
    seen,
    sums,
    folder,
    field,
    along,
    across,
    taps,
    partner_taps,
    mixer,
    given,
    own,
    got,
    coded,
    scale,
    near,
    near_scale,
    far,
    far_scale,
    side,
    side_scale,
    stack,
    base,
    early_sum,
    made,
    made_scale,
    came,
    came_scale,
    values,
    along_off,
    across_off,
    start,
    cube_sem,
    arg_sem,
    give_sent,
    give_sem,
    near_sent,
    near_sem,
    far_sent,
    far_sem,
    side_sent,
    side_sem,
    came_sent,
    came_sem,
    share_sent,
    share_sem,
):
    bands, lines, columns, ms, half, direct, line_size = sizes
    groups = lines // ROWS
    relayed = half - direct
    core = lax.axis_index("band")
    index = lax.axis_index("line")
    mine, theirs = 1 - core, core
    other = {"band": 1 - core}
    even = index % 2 == 0
    partner = {"line": index + 1 - 2 * (index % 2)}
    step = 2 - 4 * (index % 2)
    ahead, behind = index + step, index - step
    has_ahead = jnp.logical_and(ahead >= 0, ahead < line_size)
    has_behind = jnp.logical_and(behind >= 0, behind < line_size)

    chunks = []
    for size in CHUNKS:
        begin_at = chunks[-1][0] + chunks[-1][1] if chunks else 0
        chunks.append((begin_at, size))
    last_chunk = len(chunks) - 1
    spans = ((0, chunks[-1][0]), chunks[-1])
    scale_spans = ((0, last_chunk), (last_chunk, 1))
    hops = [(c, *chunks[c]) for c in range(last_chunk)]
    hops += [(last_chunk, g, 1) for g in range(chunks[-1][0], groups)]
    parts = []
    for r, count in enumerate(PARTS):
        for piece in range(count):
            parts.append((r, piece * (lines // count), lines // count))

    def remote(src, dst, sent, sem, device):
        return pltpu.make_async_remote_copy(
            src_ref=src,
            dst_ref=dst,
            send_sem=sent,
            recv_sem=sem,
            device_id=device,
            device_id_type=MESH,
        )

    def cube_copy(g, c):
        return pltpu.make_async_copy(
            cube.at[:, pl.ds(g * ROWS, ROWS), :], field.at[g], cube_sem.at[c]
        )

    def cube_starts(c):
        first_group, size = chunks[c]
        for g in range(first_group, first_group + size):
            cube_copy(g, c).start()

    def cube_wait(c):
        ref = field.at[pl.ds(*chunks[c])]
        pltpu.make_async_copy(ref, ref, cube_sem.at[c]).wait()

    def give_copy(span, c):
        span = pl.ds(*span)
        return remote(given.at[span], got.at[span], give_sent.at[0], give_sem.at[c], other)

    def near_copy(span, h):
        span = pl.ds(*span)
        return remote(
            coded.at[span, pl.ds(0, direct)], near.at[span], near_sent.at[0], near_sem.at[h], partner
        )

    def near_scale_copy(span, c):
        span = pl.ds(*span)
        return remote(
            scale.at[span], near_scale.at[span], near_sent.at[1], near_sem.at[len(hops) + c], partner
        )

    def far_copy(span, n):
        span = pl.ds(*span)
        return remote(near.at[span], far.at[span], far_sent.at[0], far_sem.at[0, n], {"line": ahead})

    def far_scale_copy(span, n):
        span = pl.ds(*span)
        return remote(
            near_scale.at[span],
            far_scale.at[span],
            far_sent.at[1],
            far_sem.at[1, n],
            {"line": ahead},
        )

    def side_copies(span, scale_span, n, count):
        span, scale_span = pl.ds(*span), pl.ds(*scale_span)
        device = {"line": behind}
        return (
            remote(
                coded.at[span, pl.ds(direct, count)],
                side.at[span, pl.ds(0, count)],
                side_sent.at[0],
                side_sem.at[0, n],
                device,
            ),
            remote(
                scale.at[scale_span],
                side_scale.at[scale_span],
                side_sent.at[1],
                side_sem.at[1, n],
                device,
            ),
        )

    def came_copies(n):
        r, top, rows = parts[n]
        kind = int(r == relayed - 1)
        return (
            remote(
                made.at[r, pl.ds(top, rows)],
                came.at[r, pl.ds(top, rows)],
                came_sent.at[0, kind],
                came_sem.at[0, n],
                partner,
            ),
            remote(
                made_scale.at[n], came_scale.at[n], came_sent.at[1, kind], came_sem.at[1, n], partner
            ),
        )

    def share_copy(place, k, top, rows):
        kind = int(k >= direct) + int(k == half - 1)
        ref = synthetic.at[place * half + k, pl.ds(top, rows)]
        return remote(ref, ref, share_sent.at[kind], share_sem.at[kind], other)

    def share_all(place, kind):
        first_k, count = ((0, direct), (direct, relayed - 1), (half - 1, 1))[kind]
        ref = synthetic.at[pl.ds(place * half + first_k, count)]
        return remote(ref, ref, share_sent.at[kind], share_sem.at[kind], other)

    def counted(body):
        if 2 * half == ms:
            body(relayed)
        else:
            whole = mine * half + half <= ms
            pl.when(whole)(lambda: body(relayed))
            pl.when(jnp.logical_not(whole))(lambda: body(relayed - 1))

    def guard(k, place, body):
        if half + k < ms:
            body()
        else:
            pl.when(place * half + k < ms)(body)

    along_copy = pltpu.make_async_copy(along_hbm, along, arg_sem.at[0])
    across_copy = pltpu.make_async_copy(across_hbm, across, arg_sem.at[1])
    seen_copy = pltpu.make_async_copy(observed, seen, arg_sem.at[2])
    early = [
        pltpu.make_async_copy(values_hbm, values, arg_sem.at[3]),
        pltpu.make_async_copy(start_hbm, start, arg_sem.at[4]),
        pltpu.make_async_copy(along_off_hbm, along_off, arg_sem.at[5]),
        pltpu.make_async_copy(across_off_hbm, across_off, arg_sem.at[6]),
    ]
    for copy in early:
        copy.start()
    for c in range(EARLY_CHUNKS):
        cube_starts(c)

    barrier = pltpu.get_barrier_semaphore()
    pl.semaphore_signal(barrier, inc=1, device_id=other, device_id_type=MESH)
    pl.semaphore_signal(barrier, inc=1, device_id=partner, device_id_type=MESH)

    @pl.when(has_ahead)
    def _():
        pl.semaphore_signal(barrier, inc=1, device_id={"line": ahead}, device_id_type=MESH)

    @pl.when(has_behind)
    def _():
        pl.semaphore_signal(barrier, inc=1, device_id={"line": behind}, device_id_type=MESH)

    for copy in early:
        copy.wait()
    for c in range(EARLY_CHUNKS, len(chunks)):
        cube_starts(c)
    along_copy.start()
    across_copy.start()
    seen_copy.start()

    lane = core * bands + iota((ms, 128), 1)
    row = iota((ms, 128), 0)
    first = jnp.zeros((ms, 128), jnp.int32)
    for m in range(ms):
        first = jnp.where(row == m, start[m], first)
    slot = lane - SPB * first
    weights = values[...].astype(F32)
    response = jnp.zeros((ms, 128), F32)
    for j in range(2 * SPB):
        response = jnp.where(slot == j, weights[:, j : j + 1], response)
    tall = 2 * half * ROWS
    picks = iota((tall, ms), 0) // ROWS
    owner = jnp.where(picks < half, theirs * half + picks, mine * half + picks - half)
    choose = (owner == iota((tall, ms), 1)).astype(BF16)
    per_row = jnp.dot(choose, response.astype(BF16), preferred_element_type=F32).astype(BF16)
    wide = bands * ROWS
    spread = (iota((128, wide), 1) // ROWS == iota((128, wide), 0)).astype(BF16)
    spread_rows = jnp.dot(per_row, spread, preferred_element_type=F32)
    same = iota((tall, wide), 0) % ROWS == iota((tall, wide), 1) % ROWS
    folder[...] = jnp.where(same, spread_rows, 0.0).astype(BF16)

    peers = 2 + has_ahead.astype(jnp.int32) + has_behind.astype(jnp.int32)

    def place(k, block, g, value):
        high, low = halves(value)
        stack[k, pl.ds(2 * block * lines + g * ROWS, ROWS), :] = high
        stack[k, pl.ds((2 * block + 1) * lines + g * ROWS, ROWS), :] = low

    def fold(c):
        first_group, size = chunks[c]
        cube_wait(c)
        for g in range(first_group, first_group + size):
            block = field[g].reshape(wide, columns)
            part = jnp.dot(folder[...], block, preferred_element_type=F32)
            part = part.reshape(2 * half, ROWS, columns)
            given[g] = part[:half]
            own[g] = part[half:]

    def encode(c):
        first_group, size = chunks[c]
        give_copy(chunks[c], c).wait_recv()
        span = pl.ds(first_group, size)
        code, unit = coded_of(own[span] + got[span], (0, 1, 2))
        coded[span] = code
        scale[c] = unit[0, 0]
        near_scale_copy((c, 1), c).start()
        for h, (at, *hop) in enumerate(hops):
            if at == c:
                near_copy(hop, h).start()

        @pl.when(has_behind)
        def _():
            @counted
            def _(count):
                for copy in side_copies(chunks[c], (c, 1), int(c == last_chunk), count):
                    copy.start()

        for g in range(first_group, first_group + size):
            value = own[g] + got[g]
            for k in range(half):
                place(k, 0, g, value[k])

    for step in ORDER.split():
        c = int(step[1:])
        if step[0] == "f":
            fold(c)
            if c == 0:
                pl.semaphore_wait(barrier, peers)
            give_copy(chunks[c], c).start()
        else:
            encode(c)

    along_copy.wait()
    across_copy.wait()
    before, after = (picked(along, along_off, -1), picked(along, along_off, 1))
    middle = picked(along, along_off, 0)
    near_tap = jnp.where(even, after, before).astype(BF16)
    far_tap = jnp.where(even, before, after).astype(BF16)
    middle = middle.astype(BF16)
    taps[...] = jnp.concatenate([middle, middle, near_tap, near_tap, far_tap, far_tap], axis=1)
    partner_taps[...] = jnp.concatenate([far_tap, far_tap, near_tap, near_tap], axis=1)
    count = columns // BLK
    mixer[...] = jnp.zeros(mixer.shape, BF16)
    for shift in (-1, 0, 1):
        turned = jnp.transpose(picked(across, across_off, shift)).astype(BF16)
        for j in range(count):
            if 0 <= j + shift < count:
                for part in range(2):
                    top = part * columns + (j + shift) * BLK
                    mixer[top : top + BLK, j * BLK : (j + 1) * BLK] = turned

    @pl.when(jnp.logical_not(has_behind))
    def _():
        stack[0:direct, 4 * lines : 6 * lines, :] = jnp.zeros((direct, 2 * lines, columns), BF16)

    @pl.when(jnp.logical_not(has_ahead))
    def _():
        stack[direct:half, 2 * lines : 4 * lines, :] = jnp.zeros((relayed, 2 * lines, columns), BF16)

    def mixed(smooth):
        both = jnp.concatenate(halves(smooth), axis=1)
        return jnp.dot(both, mixer[...], preferred_element_type=F32)

    def take_near(h):
        c, *hop = hops[h]
        opens = hop[0] == chunks[c][0]
        if opens:
            near_scale_copy((c, 1), c).wait_recv()
        near_copy(hop, h).wait_recv()

        @pl.when(has_ahead)
        def _():
            if opens:
                far_scale_copy((c, 1), int(c == last_chunk)).start()
            far_copy(hop, int(c == last_chunk)).start()

        for g in range(hop[0], sum(hop)):
            for k in range(direct):
                place(k, 1, g, value_of(near[g, k], near_scale[c]))

    def span_groups(n):
        for c, (first_group, size) in enumerate(chunks):
            if (c == last_chunk) == bool(n):
                for g in range(first_group, first_group + size):
                    yield c, g

    def take_side(n):
        @pl.when(has_ahead)
        def _():
            @counted
            def _(count):
                for copy in side_copies(spans[n], scale_spans[n], n, count):
                    copy.wait_recv()
                for c, g in span_groups(n):
                    for r in range(count):
                        place(direct + r, 1, g, value_of(side[g, r], side_scale[c]))

    def take_far(n):
        @pl.when(has_behind)
        def _():
            far_scale_copy(scale_spans[n], n).wait_recv()
            far_copy(spans[n], n).wait_recv()
            for c, g in span_groups(n):
                for k in range(direct):
                    place(k, 2, g, value_of(far[g, k], far_scale[c]))

    def make(r):
        k = direct + r

        def body():
            smooth = jnp.dot(
                partner_taps[...], stack[k, 0 : 4 * lines, :], preferred_element_type=F32
            )
            full = mixed(smooth)
            for n, (owner, top, rows) in enumerate(parts):
                if owner == r:
                    made[r, pl.ds(top, rows)], made_scale[n] = coded_of(full[top : top + rows], 0)
                    for copy in came_copies(n):
                        copy.start()

        guard(k, mine, body)

    def begin(r):
        k = direct + r

        def body():
            smooth = jnp.dot(
                taps[:, 0 : 2 * lines], stack[k, 0 : 2 * lines, :], preferred_element_type=F32
            )
            base[r] = mixed(smooth)

        guard(k, mine, body)

    def filtered(tap_columns, ks):
        first, size = tap_columns
        wide_stack = jnp.concatenate([stack[k, first : first + size, :] for k in ks], axis=1)
        smooth = jnp.dot(
            taps[:, first : first + size], wide_stack, preferred_element_type=F32
        )
        tall_smooth = jnp.concatenate(
            [smooth[:, n * columns : (n + 1) * columns] for n in range(len(ks))], axis=0
        )
        full = mixed(tall_smooth)
        return [full[n * lines : (n + 1) * lines] for n in range(len(ks))]

    def begin_direct(ks):
        for k, value in zip(ks, filtered((0, 4 * lines), ks)):
            early_sum[k] = value

    def finish_direct(ks):
        for k, value in zip(ks, filtered((4 * lines, 2 * lines), ks)):
            synthetic[mine * half + k] = early_sum[k] + value
        for k in ks:
            share_copy(mine, k, 0, lines).start()

    def finish_relayed(n):
        r, top, rows = parts[n]
        k = direct + r

        def body():
            for copy in came_copies(n):
                copy.wait_recv()
            span = pl.ds(top, rows)
            added = value_of(came[r, span], came_scale[n])
            synthetic[mine * half + k, span, :] = base[r, span, :] + added
            share_copy(mine, k, top, rows).start()

        guard(k, mine, body)

    def tally(places):
        def body(t, carry):
            rows = pl.ds(t * ROWS, ROWS)
            inner, power = sums[0, rows, :], sums[1, rows, :]
            for spot in places:
                mine = synthetic[spot, rows, :]
                inner += mine * seen[spot, rows, :].astype(F32)
                power += mine * mine
            sums[0, rows, :] = inner
            sums[1, rows, :] = power
            return carry

        lax.fori_loop(0, groups, body, 0)

    def measure(t, carry):
        rows = pl.ds(t * ROWS, ROWS)
        level = jnp.zeros((ROWS, columns), F32)
        for m in range(ms):
            sight = seen[m, rows, :].astype(F32)
            level += sight * sight
        sums[0, rows, :] = jnp.zeros((ROWS, columns), F32)
        sums[1, rows, :] = jnp.zeros((ROWS, columns), F32)
        sums[2, rows, :] = level
        return carry

    seen_copy.wait()
    lax.fori_loop(0, groups, measure, 0)
    take_near(0)
    begin(0)
    take_near(1)
    for r in range(1, relayed):
        begin(r)
    take_near(2)
    take_side(0)
    take_side(1)
    make(0)
    take_near(3)
    make(1)
    for h in range(4, len(hops)):
        take_near(h)
    for r in range(2, relayed):
        make(r)
    take_far(0)
    teams = [range(k, min(k + TEAM, direct)) for k in range(0, direct, TEAM)]
    for ks in teams:
        begin_direct(ks)
    late = [n for n in range(len(parts)) if parts[n][0] > 0]
    for n in range(len(parts)):
        if n not in late:
            finish_relayed(n)
    take_far(1)
    for ks in teams:
        finish_direct(ks)
    for n in late:
        finish_relayed(n)
    tally([mine * half + k for k in range(direct)])
    share_all(theirs, 0).wait_recv()
    tally([theirs * half + k for k in range(direct)])

    every, every_scale = (0, groups), (0, len(chunks))
    give_copy(every, 0).wait_send()
    near_copy(every, 0).wait_send()
    near_scale_copy(every_scale, 0).wait_send()

    @pl.when(has_ahead)
    def _():
        far_copy(every, 0).wait_send()
        far_scale_copy(every_scale, 0).wait_send()

    @pl.when(has_behind)
    def _():
        @counted
        def _(count):
            for copy in side_copies(every, every_scale, 0, count):
                copy.wait_send()

    def made_sent(kind):
        first, count = ((0, relayed - 1), (relayed - 1, 1))[kind]
        numbers = [n for n in range(len(parts)) if (parts[n][0] == relayed - 1) == bool(kind)]
        span, scale_span = pl.ds(first, count), pl.ds(numbers[0], len(numbers))
        remote(
            made.at[span], came.at[span], came_sent.at[0, kind], came_sem.at[0, 0], partner
        ).wait_send()
        remote(
            made_scale.at[scale_span],
            came_scale.at[scale_span],
            came_sent.at[1, kind],
            came_sem.at[1, 0],
            partner,
        ).wait_send()

    made_sent(0)
    share_all(mine, 0).wait_send()
    share_all(mine, 1).wait_send()
    share_all(theirs, 1).wait_recv()

    def last_sent():
        made_sent(1)
        share_all(mine, 2).wait_send()

    guard(half - 1, mine, last_sent)
    guard(half - 1, theirs, lambda: share_all(theirs, 2).wait_recv())


def arccos(x):
    size = jnp.abs(x)
    big = size > 0.5
    square = jnp.where(big, 0.5 - 0.5 * size, size * size)
    root = jnp.where(big, jnp.sqrt(square), size)
    poly = 4.2163199048e-2
    for term in (2.4181311049e-2, 4.5470025998e-2, 7.4953002686e-2, 1.6666752422e-1):
        poly = poly * square + term
    arc = root + root * square * poly
    angle = jnp.where(big, 2.0 * arc, 0.5 * math.pi - arc)
    return jnp.where(x < 0.0, math.pi - angle, angle)


def finish_kernel(places, synthetic, seen, sums, synthetic_out, angles_out, angles, sem):
    copy = pltpu.make_async_copy(synthetic, synthetic_out, sem.at[0])
    copy.start()

    def angle(t, carry):
        rows = pl.ds(t * ROWS, ROWS)
        inner, power, level = (sums[n, rows, :] for n in range(3))
        for spot in places:
            mine = synthetic[spot, rows, :]
            inner += mine * seen[spot, rows, :].astype(F32)
            power += mine * mine
        norm = jnp.maximum(jnp.sqrt(power) * jnp.sqrt(level), 1.0)
        angles[rows, :] = arccos(jnp.clip(inner / norm, -1.0, 1.0))
        return carry

    lax.fori_loop(0, angles.shape[0] // ROWS, angle, 0)
    last = pltpu.make_async_copy(angles, angles_out, sem.at[1])
    last.start()
    copy.wait()
    last.wait()


def on_device(
    cube,
    observed,
    along_kernels,
    along_offsets,
    across_kernels,
    across_offsets,
    resp_start,
    resp_values,
):
    bands, lines, columns = cube.shape
    ms = observed.shape[0]
    cores = lax.axis_size("band")
    line_size = lax.axis_size("line")
    assert cores == 2 and line_size % 2 == 0 and lines == BLK and bands <= 128
    half = -(-ms // cores)
    direct = (half + 1) // 2
    relayed = half - direct
    groups = lines // ROWS
    assert sum(CHUNKS) == groups and len(PARTS) == relayed and relayed > 1
    sizes = (bands, lines, columns, ms, half, direct, line_size)
    hbm = pl.BlockSpec(memory_space=pltpu.HBM)
    vmem = pl.BlockSpec(memory_space=pltpu.VMEM)
    dma = pltpu.SemaphoreType.DMA
    results = pl.pallas_call(
        functools.partial(kernel, sizes),
        out_shape=(
            pltpu.VMEM((ms, lines, columns), F32),
            pltpu.VMEM((ms, lines, columns), BF16),
            pltpu.VMEM((3, lines, columns), F32),
        ),
        in_specs=[hbm] * 8,
        out_specs=(vmem,) * 3,
        scratch_shapes=[
            pltpu.VMEM((2 * half * ROWS, bands * ROWS), BF16),
            pltpu.VMEM((groups, bands, ROWS, columns), BF16),
            pltpu.VMEM((3, BLK, BLK), BF16),
            pltpu.VMEM((3, BLK, BLK), BF16),
            pltpu.VMEM((BLK, 6 * BLK), BF16),
            pltpu.VMEM((BLK, 4 * BLK), BF16),
            pltpu.VMEM((2 * columns, columns), BF16),
            pltpu.VMEM((groups, half, ROWS, columns), F32),
            pltpu.VMEM((groups, half, ROWS, columns), F32),
            pltpu.VMEM((groups, half, ROWS, columns), F32),
            pltpu.VMEM((groups, half, ROWS, columns), I16),
            pltpu.VMEM((len(CHUNKS), 1, columns), F32),
            pltpu.VMEM((groups, direct, ROWS, columns), I16),
            pltpu.VMEM((len(CHUNKS), 1, columns), F32),
            pltpu.VMEM((groups, direct, ROWS, columns), I16),
            pltpu.VMEM((len(CHUNKS), 1, columns), F32),
            pltpu.VMEM((groups, relayed, ROWS, columns), I16),
            pltpu.VMEM((len(CHUNKS), 1, columns), F32),
            pltpu.VMEM((half, 6 * lines, columns), BF16),
            pltpu.VMEM((relayed, lines, columns), F32),
            pltpu.VMEM((direct, lines, columns), F32),
            pltpu.VMEM((relayed, lines, columns), I16),
            pltpu.VMEM((sum(PARTS), 1, columns), F32),
            pltpu.VMEM((relayed, lines, columns), I16),
            pltpu.VMEM((sum(PARTS), 1, columns), F32),
            pltpu.VMEM(resp_values.shape, BF16),
            pltpu.SMEM(along_offsets.shape, jnp.int32),
            pltpu.SMEM(across_offsets.shape, jnp.int32),
            pltpu.SMEM(resp_start.shape, jnp.int32),
            dma((len(CHUNKS),)),
            dma((7,)),
            dma((1,)),
            dma((len(CHUNKS),)),
            dma((2,)),
            dma((2 * len(CHUNKS) + CHUNKS[-1] - 1,)),
            dma((2,)),
            dma((2, 2)),
            dma((2,)),
            dma((2, 2)),
            dma((2, 2)),
            dma((2, sum(PARTS))),
            dma((3,)),
            dma((3,)),
        ],
        compiler_params=pltpu.CompilerParams(
            collective_id=0, has_side_effects=True, vmem_limit_bytes=48_000_000
        ),
    )(
        *(
            pltpu.with_memory_space_constraint(value, pltpu.HBM)
            for value in (
                cube,
                observed,
                along_kernels,
                across_kernels,
                resp_values,
                along_offsets,
                across_offsets,
                resp_start,
            )
        )
    )
    places = [m for m in range(ms) if m % half >= direct]
    return pl.pallas_call(
        functools.partial(finish_kernel, places),
        out_shape=(
            jax.ShapeDtypeStruct((ms, lines, columns), F32),
            jax.ShapeDtypeStruct((lines, columns), F32),
        ),
        in_specs=[vmem] * 3,
        out_specs=(hbm, hbm),
        scratch_shapes=[pltpu.VMEM((lines, columns), F32), dma((2,))],
        compiler_params=pltpu.CompilerParams(vmem_limit_bytes=8_000_000),
    )(*(pltpu.with_memory_space_constraint(value, pltpu.VMEM) for value in results))


def solution(mesh):
    placed = (
        P("band", ("slab", "line"), None),
        P(None, ("slab", "line"), None),
        P(),
        P(),
        P(),
        P(),
        P(),
        P(),
    )
    return jax.shard_map(
        on_device,
        mesh=mesh,
        in_specs=placed,
        out_specs=(P(None, ("slab", "line"), None), P(("slab", "line"), None)),
        check_vma=False,
    )
```

```python
import functools
import math

import jax
import jax.numpy as jnp
from jax import lax
from jax.experimental import pallas as pl
from jax.experimental.pallas import tpu as pltpu
from jax.sharding import PartitionSpec as P

BLK = 128
SPB = 10
ROWS = 16
EARLY_CHUNKS = 3
CHUNKS = (1, 1, 2, 2, 2)
FOLD, CODE = 0, 1
ORDER = (
    (FOLD, 0),
    (FOLD, 1),
    (FOLD, 2),
    (CODE, 0),
    (CODE, 1),
    (FOLD, 3),
    (CODE, 2),
    (FOLD, 4),
    (CODE, 3),
    (CODE, 4),
)
PARTS = (1, 1, 1)
TEAM = 2
MESH = pl.DeviceIdType.MESH
F32 = jnp.float32
BF16 = jnp.bfloat16
I16 = jnp.int16
PEAK = 32767.0


def halves(value):
    high = value.astype(BF16)
    low = (value - high.astype(F32)).astype(BF16)
    return high, low


def coded_of(value, axes):
    peak = jnp.max(jnp.abs(value), axis=axes, keepdims=True)
    inverse = jnp.where(peak > 0.0, PEAK / jnp.maximum(peak, 1e-30), 0.0)
    code = jnp.round(value * inverse).astype(jnp.int32).astype(I16)
    return code, peak * (1.0 / PEAK)


def value_of(code, scale):
    return code.astype(jnp.int32).astype(F32) * scale


def picked(kernels, offsets, shift):
    total = None
    for k in range(3):
        term = jnp.where(offsets[k] == shift, kernels[k].astype(F32), 0.0)
        total = term if total is None else total + term
    return total


def iota(shape, dim):
    return lax.broadcasted_iota(jnp.int32, shape, dim)


def kernel(
    sizes,
    cube,
    observed,
    along_hbm,
    across_hbm,
    values_hbm,
    along_off_hbm,
    across_off_hbm,
    start_hbm,
    synthetic,
    seen,
    power_seen,
    folder,
    field,
    along,
    across,
    taps,
    partner_taps,
    mixer,
    given,
    own,
    got,
    coded,
    scale,
    near,
    near_scale,
    far,
    far_scale,
    side,
    side_scale,
    stack,
    base,
    early_sum,
    made,
    made_scale,
    came,
    came_scale,
    values,
    along_off,
    across_off,
    start,
    cube_sem,
    arg_sem,
    give_sent,
    give_sem,
    near_sent,
    near_sem,
    far_sent,
    far_sem,
    side_sent,
    side_sem,
    came_sent,
    came_sem,
    share_sent,
    share_sem,
):
    bands, lines, columns, ms, half, direct, line_size = sizes
    groups = lines // ROWS
    relayed = half - direct
    core = lax.axis_index("band")
    index = lax.axis_index("line")
    mine, theirs = 1 - core, core
    other = {"band": 1 - core}
    even = index % 2 == 0
    partner = {"line": index + 1 - 2 * (index % 2)}
    step = 2 - 4 * (index % 2)
    ahead, behind = index + step, index - step
    has_ahead = jnp.logical_and(ahead >= 0, ahead < line_size)
    has_behind = jnp.logical_and(behind >= 0, behind < line_size)

    chunks = []
    for size in CHUNKS:
        begin_at = chunks[-1][0] + chunks[-1][1] if chunks else 0
        chunks.append((begin_at, size))
    last_chunk = len(chunks) - 1
    spans = ((0, chunks[-1][0]), chunks[-1])
    scale_spans = ((0, last_chunk), (last_chunk, 1))
    hops = [(c, *chunks[c]) for c in range(last_chunk)]
    hops += [(last_chunk, g, 1) for g in range(chunks[-1][0], groups)]
    parts = []
    for r, count in enumerate(PARTS):
        for piece in range(count):
            parts.append((r, piece * (lines // count), lines // count))

    def remote(src, dst, sent, sem, device):
        return pltpu.make_async_remote_copy(
            src_ref=src,
            dst_ref=dst,
            send_sem=sent,
            recv_sem=sem,
            device_id=device,
            device_id_type=MESH,
        )

    def cube_copy(g, c):
        return pltpu.make_async_copy(
            cube.at[:, pl.ds(g * ROWS, ROWS), :], field.at[g], cube_sem.at[c]
        )

    def cube_starts(c):
        first_group, size = chunks[c]
        for g in range(first_group, first_group + size):
            cube_copy(g, c).start()

    def cube_wait(c):
        ref = field.at[pl.ds(*chunks[c])]
        pltpu.make_async_copy(ref, ref, cube_sem.at[c]).wait()

    def give_copy(span, c):
        span = pl.ds(*span)
        return remote(given.at[span], got.at[span], give_sent.at[0], give_sem.at[c], other)

    def near_copy(span, h):
        span = pl.ds(*span)
        return remote(
            coded.at[span, pl.ds(0, direct)], near.at[span], near_sent.at[0], near_sem.at[h], partner
        )

    def near_scale_copy(span, c):
        span = pl.ds(*span)
        return remote(
            scale.at[span], near_scale.at[span], near_sent.at[1], near_sem.at[len(hops) + c], partner
        )

    def far_copy(span, n):
        span = pl.ds(*span)
        return remote(near.at[span], far.at[span], far_sent.at[0], far_sem.at[0, n], {"line": ahead})

    def far_scale_copy(span, n):
        span = pl.ds(*span)
        return remote(
            near_scale.at[span],
            far_scale.at[span],
            far_sent.at[1],
            far_sem.at[1, n],
            {"line": ahead},
        )

    def side_copies(span, scale_span, n, count):
        span, scale_span = pl.ds(*span), pl.ds(*scale_span)
        device = {"line": behind}
        return (
            remote(
                coded.at[span, pl.ds(direct, count)],
                side.at[span, pl.ds(0, count)],
                side_sent.at[0],
                side_sem.at[0, n],
                device,
            ),
            remote(
                scale.at[scale_span],
                side_scale.at[scale_span],
                side_sent.at[1],
                side_sem.at[1, n],
                device,
            ),
        )

    def came_copies(n):
        r, top, rows = parts[n]
        kind = int(r == relayed - 1)
        return (
            remote(
                made.at[r, pl.ds(top, rows)],
                came.at[r, pl.ds(top, rows)],
                came_sent.at[0, kind],
                came_sem.at[0, n],
                partner,
            ),
            remote(
                made_scale.at[n], came_scale.at[n], came_sent.at[1, kind], came_sem.at[1, n], partner
            ),
        )

    def share_copy(place, k, top, rows):
        kind = int(k >= direct) + int(k == half - 1)
        ref = synthetic.at[place * half + k, pl.ds(top, rows)]
        return remote(ref, ref, share_sent.at[kind], share_sem.at[kind], other)

    def share_all(place, kind):
        first_k, count = ((0, direct), (direct, relayed - 1), (half - 1, 1))[kind]
        ref = synthetic.at[pl.ds(place * half + first_k, count)]
        return remote(ref, ref, share_sent.at[kind], share_sem.at[kind], other)

    def counted(body):
        if 2 * half == ms:
            body(relayed)
        else:
            whole = mine * half + half <= ms
            pl.when(whole)(lambda: body(relayed))
            pl.when(jnp.logical_not(whole))(lambda: body(relayed - 1))

    def guard(k, place, body):
        if half + k < ms:
            body()
        else:
            pl.when(place * half + k < ms)(body)

    along_copy = pltpu.make_async_copy(along_hbm, along, arg_sem.at[0])
    across_copy = pltpu.make_async_copy(across_hbm, across, arg_sem.at[1])
    seen_copy = pltpu.make_async_copy(observed, seen, arg_sem.at[2])
    early = [
        pltpu.make_async_copy(values_hbm, values, arg_sem.at[3]),
        pltpu.make_async_copy(start_hbm, start, arg_sem.at[4]),
        pltpu.make_async_copy(along_off_hbm, along_off, arg_sem.at[5]),
        pltpu.make_async_copy(across_off_hbm, across_off, arg_sem.at[6]),
    ]
    for copy in early:
        copy.start()
    for c in range(EARLY_CHUNKS):
        cube_starts(c)

    barrier = pltpu.get_barrier_semaphore()
    pl.semaphore_signal(barrier, inc=1, device_id=other, device_id_type=MESH)
    pl.semaphore_signal(barrier, inc=1, device_id=partner, device_id_type=MESH)

    @pl.when(has_ahead)
    def _():
        pl.semaphore_signal(barrier, inc=1, device_id={"line": ahead}, device_id_type=MESH)

    @pl.when(has_behind)
    def _():
        pl.semaphore_signal(barrier, inc=1, device_id={"line": behind}, device_id_type=MESH)

    for copy in early:
        copy.wait()
    for c in range(EARLY_CHUNKS, len(chunks)):
        cube_starts(c)
    along_copy.start()
    across_copy.start()
    seen_copy.start()

    lane = core * bands + iota((ms, 128), 1)
    row = iota((ms, 128), 0)
    first = jnp.zeros((ms, 128), jnp.int32)
    for m in range(ms):
        first = jnp.where(row == m, start[m], first)
    slot = lane - SPB * first
    weights = values[...].astype(F32)
    response = jnp.zeros((ms, 128), F32)
    for j in range(2 * SPB):
        response = jnp.where(slot == j, weights[:, j : j + 1], response)
    tall = 2 * half * ROWS
    picks = iota((tall, ms), 0) // ROWS
    owner = jnp.where(picks < half, theirs * half + picks, mine * half + picks - half)
    choose = (owner == iota((tall, ms), 1)).astype(BF16)
    per_row = jnp.dot(choose, response.astype(BF16), preferred_element_type=F32).astype(BF16)
    wide = bands * ROWS
    spread = (iota((128, wide), 1) // ROWS == iota((128, wide), 0)).astype(BF16)
    spread_rows = jnp.dot(per_row, spread, preferred_element_type=F32)
    same = iota((tall, wide), 0) % ROWS == iota((tall, wide), 1) % ROWS
    folder[...] = jnp.where(same, spread_rows, 0.0).astype(BF16)

    peers = 2 + has_ahead.astype(jnp.int32) + has_behind.astype(jnp.int32)

    def place(k, block, g, value):
        high, low = halves(value)
        stack[k, pl.ds(2 * block * lines + g * ROWS, ROWS), :] = high
        stack[k, pl.ds((2 * block + 1) * lines + g * ROWS, ROWS), :] = low

    def fold(c):
        first_group, size = chunks[c]
        cube_wait(c)
        for g in range(first_group, first_group + size):
            block = field[g].reshape(wide, columns)
            part = jnp.dot(folder[...], block, preferred_element_type=F32)
            part = part.reshape(2 * half, ROWS, columns)
            given[g] = part[:half]
            own[g] = part[half:]

    def encode(c):
        first_group, size = chunks[c]
        give_copy(chunks[c], c).wait_recv()
        span = pl.ds(first_group, size)
        code, unit = coded_of(own[span] + got[span], (0, 1, 2))
        coded[span] = code
        scale[c] = unit[0, 0]
        near_scale_copy((c, 1), c).start()
        for h, (at, *hop) in enumerate(hops):
            if at == c:
                near_copy(hop, h).start()

        @pl.when(has_behind)
        def _():
            @counted
            def _(count):
                for copy in side_copies(chunks[c], (c, 1), int(c == last_chunk), count):
                    copy.start()

        for g in range(first_group, first_group + size):
            value = own[g] + got[g]
            for k in range(half):
                place(k, 0, g, value[k])

    for step, c in ORDER:
        if step == FOLD:
            fold(c)
            if c == 0:
                pl.semaphore_wait(barrier, peers)
            give_copy(chunks[c], c).start()
        else:
            encode(c)

    along_copy.wait()
    across_copy.wait()
    before, after = (picked(along, along_off, -1), picked(along, along_off, 1))
    middle = picked(along, along_off, 0)
    near_tap = jnp.where(even, after, before).astype(BF16)
    far_tap = jnp.where(even, before, after).astype(BF16)
    middle = middle.astype(BF16)
    taps[...] = jnp.concatenate([middle, middle, near_tap, near_tap, far_tap, far_tap], axis=1)
    partner_taps[...] = jnp.concatenate([far_tap, far_tap, near_tap, near_tap], axis=1)
    count = columns // BLK
    mixer[...] = jnp.zeros(mixer.shape, BF16)
    for shift in (-1, 0, 1):
        turned = jnp.transpose(picked(across, across_off, shift)).astype(BF16)
        for j in range(count):
            if 0 <= j + shift < count:
                for part in range(2):
                    top = part * columns + (j + shift) * BLK
                    mixer[top : top + BLK, j * BLK : (j + 1) * BLK] = turned

    @pl.when(jnp.logical_not(has_behind))
    def _():
        stack[0:direct, 4 * lines : 6 * lines, :] = jnp.zeros((direct, 2 * lines, columns), BF16)

    @pl.when(jnp.logical_not(has_ahead))
    def _():
        stack[direct:half, 2 * lines : 4 * lines, :] = jnp.zeros((relayed, 2 * lines, columns), BF16)

    def mixed(smooth):
        both = jnp.concatenate(halves(smooth), axis=1)
        return jnp.dot(both, mixer[...], preferred_element_type=F32)

    def take_near(h):
        c, *hop = hops[h]
        opens = hop[0] == chunks[c][0]
        if opens:
            near_scale_copy((c, 1), c).wait_recv()
        near_copy(hop, h).wait_recv()

        @pl.when(has_ahead)
        def _():
            if opens:
                far_scale_copy((c, 1), int(c == last_chunk)).start()
            far_copy(hop, int(c == last_chunk)).start()

        for g in range(hop[0], sum(hop)):
            for k in range(direct):
                place(k, 1, g, value_of(near[g, k], near_scale[c]))

    def span_groups(n):
        for c, (first_group, size) in enumerate(chunks):
            if (c == last_chunk) == bool(n):
                for g in range(first_group, first_group + size):
                    yield c, g

    def take_side(n):
        @pl.when(has_ahead)
        def _():
            @counted
            def _(count):
                for copy in side_copies(spans[n], scale_spans[n], n, count):
                    copy.wait_recv()
                for c, g in span_groups(n):
                    for r in range(count):
                        place(direct + r, 1, g, value_of(side[g, r], side_scale[c]))

    def take_far(n):
        @pl.when(has_behind)
        def _():
            far_scale_copy(scale_spans[n], n).wait_recv()
            far_copy(spans[n], n).wait_recv()
            for c, g in span_groups(n):
                for k in range(direct):
                    place(k, 2, g, value_of(far[g, k], far_scale[c]))

    def make(r):
        k = direct + r

        def body():
            smooth = jnp.dot(
                partner_taps[...], stack[k, 0 : 4 * lines, :], preferred_element_type=F32
            )
            full = mixed(smooth)
            for n, (owner, top, rows) in enumerate(parts):
                if owner == r:
                    made[r, pl.ds(top, rows)], made_scale[n] = coded_of(full[top : top + rows], 0)
                    for copy in came_copies(n):
                        copy.start()

        guard(k, mine, body)

    def begin(r):
        k = direct + r

        def body():
            smooth = jnp.dot(
                taps[:, 0 : 2 * lines], stack[k, 0 : 2 * lines, :], preferred_element_type=F32
            )
            base[r] = mixed(smooth)

        guard(k, mine, body)

    def filtered(tap_columns, ks):
        first, size = tap_columns
        wide_stack = jnp.concatenate([stack[k, first : first + size, :] for k in ks], axis=1)
        smooth = jnp.dot(
            taps[:, first : first + size], wide_stack, preferred_element_type=F32
        )
        tall_smooth = jnp.concatenate(
            [smooth[:, n * columns : (n + 1) * columns] for n in range(len(ks))], axis=0
        )
        full = mixed(tall_smooth)
        return [full[n * lines : (n + 1) * lines] for n in range(len(ks))]

    def begin_direct(ks):
        for k, value in zip(ks, filtered((0, 4 * lines), ks)):
            early_sum[k] = value

    def finish_direct(ks):
        for k, value in zip(ks, filtered((4 * lines, 2 * lines), ks)):
            synthetic[mine * half + k] = early_sum[k] + value
        for k in ks:
            share_copy(mine, k, 0, lines).start()

    def finish_relayed(n):
        r, top, rows = parts[n]
        k = direct + r

        def body():
            for copy in came_copies(n):
                copy.wait_recv()
            span = pl.ds(top, rows)
            added = value_of(came[r, span], came_scale[n])
            synthetic[mine * half + k, span, :] = base[r, span, :] + added
            share_copy(mine, k, top, rows).start()

        guard(k, mine, body)

    def measure(t, carry):
        rows = pl.ds(t * ROWS, ROWS)
        level = jnp.zeros((ROWS, columns), F32)
        for m in range(ms):
            sight = seen[m, rows, :].astype(F32)
            level += sight * sight
        power_seen[rows, :] = level
        return carry

    seen_copy.wait()
    lax.fori_loop(0, groups, measure, 0)
    take_near(0)
    begin(0)
    take_near(1)
    for r in range(1, relayed):
        begin(r)
    take_near(2)
    take_side(0)
    take_side(1)
    make(0)
    take_near(3)
    make(1)
    for h in range(4, len(hops)):
        take_near(h)
    for r in range(2, relayed):
        make(r)
    teams = [range(k, min(k + TEAM, direct)) for k in range(0, direct, TEAM)]
    late = [n for n in range(len(parts)) if parts[n][0] > 0]
    for ks in teams:
        begin_direct(ks)
    take_far(0)
    for n in range(len(parts)):
        if n not in late:
            finish_relayed(n)
    take_far(1)
    for ks in teams:
        finish_direct(ks)
    for n in late:
        finish_relayed(n)
    share_all(theirs, 0).wait_recv()

    every, every_scale = (0, groups), (0, len(chunks))
    give_copy(every, 0).wait_send()
    near_copy(every, 0).wait_send()
    near_scale_copy(every_scale, 0).wait_send()

    @pl.when(has_ahead)
    def _():
        far_copy(every, 0).wait_send()
        far_scale_copy(every_scale, 0).wait_send()

    @pl.when(has_behind)
    def _():
        @counted
        def _(count):
            for copy in side_copies(every, every_scale, 0, count):
                copy.wait_send()

    def made_sent(kind):
        first, count = ((0, relayed - 1), (relayed - 1, 1))[kind]
        numbers = [n for n in range(len(parts)) if (parts[n][0] == relayed - 1) == bool(kind)]
        span, scale_span = pl.ds(first, count), pl.ds(numbers[0], len(numbers))
        remote(
            made.at[span], came.at[span], came_sent.at[0, kind], came_sem.at[0, 0], partner
        ).wait_send()
        remote(
            made_scale.at[scale_span],
            came_scale.at[scale_span],
            came_sent.at[1, kind],
            came_sem.at[1, 0],
            partner,
        ).wait_send()

    made_sent(0)
    share_all(mine, 0).wait_send()
    share_all(mine, 1).wait_send()
    share_all(theirs, 1).wait_recv()

    def last_sent():
        made_sent(1)
        share_all(mine, 2).wait_send()

    guard(half - 1, mine, last_sent)
    guard(half - 1, theirs, lambda: share_all(theirs, 2).wait_recv())


def arccos(x):
    size = jnp.abs(x)
    big = size > 0.5
    square = jnp.where(big, 0.5 - 0.5 * size, size * size)
    root = jnp.where(big, jnp.sqrt(square), size)
    poly = 4.2163199048e-2
    for term in (2.4181311049e-2, 4.5470025998e-2, 7.4953002686e-2, 1.6666752422e-1):
        poly = poly * square + term
    arc = root + root * square * poly
    angle = jnp.where(big, 2.0 * arc, 0.5 * math.pi - arc)
    return jnp.where(x < 0.0, math.pi - angle, angle)


def finish_kernel(synthetic, seen, power_seen, synthetic_out, angles_out, angles, sem):
    copy = pltpu.make_async_copy(synthetic, synthetic_out, sem.at[0])
    copy.start()

    def angle(t, carry):
        rows = pl.ds(t * ROWS, ROWS)
        inner = power = jnp.zeros((ROWS, angles.shape[1]), F32)
        for m in range(synthetic.shape[0]):
            value = synthetic[m, rows, :]
            inner += value * seen[m, rows, :].astype(F32)
            power += value * value
        norm = jnp.maximum(jnp.sqrt(power) * jnp.sqrt(power_seen[rows, :]), 1.0)
        angles[rows, :] = arccos(jnp.clip(inner / norm, -1.0, 1.0))
        return carry

    lax.fori_loop(0, angles.shape[0] // ROWS, angle, 0, unroll=True)
    last = pltpu.make_async_copy(angles, angles_out, sem.at[1])
    last.start()
    copy.wait()
    last.wait()


def on_device(
    cube,
    observed,
    along_kernels,
    along_offsets,
    across_kernels,
    across_offsets,
    resp_start,
    resp_values,
):
    bands, lines, columns = cube.shape
    ms = observed.shape[0]
    cores = lax.axis_size("band")
    line_size = lax.axis_size("line")
    assert cores == 2 and line_size % 2 == 0 and lines == BLK and bands <= 128
    half = -(-ms // cores)
    direct = (half + 1) // 2
    relayed = half - direct
    groups = lines // ROWS
    assert sum(CHUNKS) == groups and len(PARTS) == relayed and relayed > 1
    sizes = (bands, lines, columns, ms, half, direct, line_size)
    hbm = pl.BlockSpec(memory_space=pltpu.HBM)
    vmem = pl.BlockSpec(memory_space=pltpu.VMEM)
    dma = pltpu.SemaphoreType.DMA
    results = pl.pallas_call(
        functools.partial(kernel, sizes),
        out_shape=(
            pltpu.VMEM((ms, lines, columns), F32),
            pltpu.VMEM((ms, lines, columns), BF16),
            pltpu.VMEM((lines, columns), F32),
        ),
        in_specs=[hbm] * 8,
        out_specs=(vmem,) * 3,
        scratch_shapes=[
            pltpu.VMEM((2 * half * ROWS, bands * ROWS), BF16),
            pltpu.VMEM((groups, bands, ROWS, columns), BF16),
            pltpu.VMEM((3, BLK, BLK), BF16),
            pltpu.VMEM((3, BLK, BLK), BF16),
            pltpu.VMEM((BLK, 6 * BLK), BF16),
            pltpu.VMEM((BLK, 4 * BLK), BF16),
            pltpu.VMEM((2 * columns, columns), BF16),
            pltpu.VMEM((groups, half, ROWS, columns), F32),
            pltpu.VMEM((groups, half, ROWS, columns), F32),
            pltpu.VMEM((groups, half, ROWS, columns), F32),
            pltpu.VMEM((groups, half, ROWS, columns), I16),
            pltpu.VMEM((len(CHUNKS), 1, columns), F32),
            pltpu.VMEM((groups, direct, ROWS, columns), I16),
            pltpu.VMEM((len(CHUNKS), 1, columns), F32),
            pltpu.VMEM((groups, direct, ROWS, columns), I16),
            pltpu.VMEM((len(CHUNKS), 1, columns), F32),
            pltpu.VMEM((groups, relayed, ROWS, columns), I16),
            pltpu.VMEM((len(CHUNKS), 1, columns), F32),
            pltpu.VMEM((half, 6 * lines, columns), BF16),
            pltpu.VMEM((relayed, lines, columns), F32),
            pltpu.VMEM((direct, lines, columns), F32),
            pltpu.VMEM((relayed, lines, columns), I16),
            pltpu.VMEM((sum(PARTS), 1, columns), F32),
            pltpu.VMEM((relayed, lines, columns), I16),
            pltpu.VMEM((sum(PARTS), 1, columns), F32),
            pltpu.VMEM(resp_values.shape, BF16),
            pltpu.SMEM(along_offsets.shape, jnp.int32),
            pltpu.SMEM(across_offsets.shape, jnp.int32),
            pltpu.SMEM(resp_start.shape, jnp.int32),
            dma((len(CHUNKS),)),
            dma((7,)),
            dma((1,)),
            dma((len(CHUNKS),)),
            dma((2,)),
            dma((2 * len(CHUNKS) + CHUNKS[-1] - 1,)),
            dma((2,)),
            dma((2, 2)),
            dma((2,)),
            dma((2, 2)),
            dma((2, 2)),
            dma((2, sum(PARTS))),
            dma((3,)),
            dma((3,)),
        ],
        compiler_params=pltpu.CompilerParams(
            collective_id=0, has_side_effects=True, vmem_limit_bytes=48_000_000
        ),
    )(
        *(
            pltpu.with_memory_space_constraint(value, pltpu.HBM)
            for value in (
                cube,
                observed,
                along_kernels,
                across_kernels,
                resp_values,
                along_offsets,
                across_offsets,
                resp_start,
            )
        )
    )
    return pl.pallas_call(
        finish_kernel,
        out_shape=(
            jax.ShapeDtypeStruct((ms, lines, columns), F32),
            jax.ShapeDtypeStruct((lines, columns), F32),
        ),
        in_specs=[vmem] * 3,
        out_specs=(hbm, hbm),
        scratch_shapes=[pltpu.VMEM((lines, columns), F32), dma((2,))],
        compiler_params=pltpu.CompilerParams(vmem_limit_bytes=8_000_000),
    )(*(pltpu.with_memory_space_constraint(value, pltpu.VMEM) for value in results))


def solution(mesh):
    placed = (
        P("band", ("slab", "line"), None),
        P(None, ("slab", "line"), None),
        P(),
        P(),
        P(),
        P(),
        P(),
        P(),
    )
    return jax.shard_map(
        on_device,
        mesh=mesh,
        in_specs=placed,
        out_specs=(P(None, ("slab", "line"), None), P(("slab", "line"), None)),
        check_vma=False,
    )
```

```python
import functools
import math

import jax
import jax.numpy as jnp
from jax import lax
from jax.experimental import pallas as pl
from jax.experimental.pallas import tpu as pltpu
from jax.sharding import PartitionSpec as P

BLK = 128
SPB = 10
ROWS = 16
EARLY_CHUNKS = 3
CHUNKS = (1, 1, 2, 2, 2)
FOLD, CODE = 0, 1
ORDER = (
    (FOLD, 0),
    (FOLD, 1),
    (FOLD, 2),
    (CODE, 0),
    (CODE, 1),
    (FOLD, 3),
    (CODE, 2),
    (FOLD, 4),
    (CODE, 3),
    (CODE, 4),
)
PARTS = (1, 1, 1)
TEAM = 4
MESH = pl.DeviceIdType.MESH
F32 = jnp.float32
BF16 = jnp.bfloat16
I16 = jnp.int16
PEAK = 32767.0


def halves(value):
    high = value.astype(BF16)
    low = (value - high.astype(F32)).astype(BF16)
    return high, low


def coded_of(value, axes):
    peak = jnp.max(jnp.abs(value), axis=axes, keepdims=True)
    inverse = jnp.where(peak > 0.0, PEAK / jnp.maximum(peak, 1e-30), 0.0)
    code = jnp.round(value * inverse).astype(jnp.int32).astype(I16)
    return code, peak * (1.0 / PEAK)


def value_of(code, scale):
    return code.astype(jnp.int32).astype(F32) * scale


def picked(kernels, offsets, shift):
    total = None
    for k in range(3):
        term = jnp.where(offsets[k] == shift, kernels[k].astype(F32), 0.0)
        total = term if total is None else total + term
    return total


def iota(shape, dim):
    return lax.broadcasted_iota(jnp.int32, shape, dim)


def kernel(
    sizes,
    cube,
    observed,
    along_hbm,
    across_hbm,
    values_hbm,
    along_off_hbm,
    across_off_hbm,
    start_hbm,
    synthetic,
    seen,
    power_seen,
    folder,
    spread,
    same,
    field,
    along,
    across,
    taps,
    partner_taps,
    mixer,
    given,
    own,
    got,
    coded,
    scale,
    near,
    near_scale,
    far,
    far_scale,
    side,
    side_scale,
    stack,
    base,
    early_sum,
    made,
    made_scale,
    came,
    came_scale,
    values,
    along_off,
    across_off,
    start,
    cube_sem,
    arg_sem,
    give_sent,
    give_sem,
    near_sent,
    near_sem,
    far_sent,
    far_sem,
    side_sent,
    side_sem,
    came_sent,
    came_sem,
    share_sent,
    share_sem,
):
    bands, lines, columns, ms, half, direct, line_size = sizes
    groups = lines // ROWS
    relayed = half - direct
    core = lax.axis_index("band")
    index = lax.axis_index("line")
    mine, theirs = 1 - core, core
    other = {"band": 1 - core}
    even = index % 2 == 0
    partner = {"line": index + 1 - 2 * (index % 2)}
    step = 2 - 4 * (index % 2)
    ahead, behind = index + step, index - step
    has_ahead = jnp.logical_and(ahead >= 0, ahead < line_size)
    has_behind = jnp.logical_and(behind >= 0, behind < line_size)

    chunks = []
    for size in CHUNKS:
        begin_at = chunks[-1][0] + chunks[-1][1] if chunks else 0
        chunks.append((begin_at, size))
    last_chunk = len(chunks) - 1
    spans = ((0, chunks[-1][0]), chunks[-1])
    scale_spans = ((0, last_chunk), (last_chunk, 1))
    hops = [(c, *chunks[c]) for c in range(last_chunk)]
    hops += [(last_chunk, g, 1) for g in range(chunks[-1][0], groups)]
    parts = []
    for r, count in enumerate(PARTS):
        for piece in range(count):
            parts.append((r, piece * (lines // count), lines // count))

    def remote(src, dst, sent, sem, device):
        return pltpu.make_async_remote_copy(
            src_ref=src,
            dst_ref=dst,
            send_sem=sent,
            recv_sem=sem,
            device_id=device,
            device_id_type=MESH,
        )

    def cube_copy(g, c):
        return pltpu.make_async_copy(
            cube.at[:, pl.ds(g * ROWS, ROWS), :], field.at[g], cube_sem.at[c]
        )

    def cube_starts(c):
        first_group, size = chunks[c]
        for g in range(first_group, first_group + size):
            cube_copy(g, c).start()

    def cube_wait(c):
        ref = field.at[pl.ds(*chunks[c])]
        pltpu.make_async_copy(ref, ref, cube_sem.at[c]).wait()

    def give_copy(span, c):
        span = pl.ds(*span)
        return remote(given.at[span], got.at[span], give_sent.at[0], give_sem.at[c], other)

    def near_copy(span, h):
        span = pl.ds(*span)
        return remote(
            coded.at[span, pl.ds(0, direct)], near.at[span], near_sent.at[0], near_sem.at[h], partner
        )

    def near_scale_copy(span, c):
        span = pl.ds(*span)
        return remote(
            scale.at[span], near_scale.at[span], near_sent.at[1], near_sem.at[len(hops) + c], partner
        )

    def far_copy(span, n):
        span = pl.ds(*span)
        return remote(near.at[span], far.at[span], far_sent.at[0], far_sem.at[0, n], {"line": ahead})

    def far_scale_copy(span, n):
        span = pl.ds(*span)
        return remote(
            near_scale.at[span],
            far_scale.at[span],
            far_sent.at[1],
            far_sem.at[1, n],
            {"line": ahead},
        )

    def side_copies(span, scale_span, n, count):
        span, scale_span = pl.ds(*span), pl.ds(*scale_span)
        device = {"line": behind}
        return (
            remote(
                coded.at[span, pl.ds(direct, count)],
                side.at[span, pl.ds(0, count)],
                side_sent.at[0],
                side_sem.at[0, n],
                device,
            ),
            remote(
                scale.at[scale_span],
                side_scale.at[scale_span],
                side_sent.at[1],
                side_sem.at[1, n],
                device,
            ),
        )

    def came_copies(n):
        r, top, rows = parts[n]
        kind = int(r == relayed - 1)
        return (
            remote(
                made.at[r, pl.ds(top, rows)],
                came.at[r, pl.ds(top, rows)],
                came_sent.at[0, kind],
                came_sem.at[0, n],
                partner,
            ),
            remote(
                made_scale.at[n], came_scale.at[n], came_sent.at[1, kind], came_sem.at[1, n], partner
            ),
        )

    def share_copy(place, k, top, rows):
        kind = int(k >= direct) + int(k == half - 1)
        ref = synthetic.at[place * half + k, pl.ds(top, rows)]
        return remote(ref, ref, share_sent.at[kind], share_sem.at[kind], other)

    def share_all(place, kind):
        first_k, count = ((0, direct), (direct, relayed - 1), (half - 1, 1))[kind]
        ref = synthetic.at[pl.ds(place * half + first_k, count)]
        return remote(ref, ref, share_sent.at[kind], share_sem.at[kind], other)

    def counted(body):
        if 2 * half == ms:
            body(relayed)
        else:
            whole = mine * half + half <= ms
            pl.when(whole)(lambda: body(relayed))
            pl.when(jnp.logical_not(whole))(lambda: body(relayed - 1))

    def guard(k, place, body):
        if half + k < ms:
            body()
        else:
            pl.when(place * half + k < ms)(body)

    along_copy = pltpu.make_async_copy(along_hbm, along, arg_sem.at[0])
    across_copy = pltpu.make_async_copy(across_hbm, across, arg_sem.at[1])
    seen_copy = pltpu.make_async_copy(observed, seen, arg_sem.at[2])
    early = [
        pltpu.make_async_copy(values_hbm, values, arg_sem.at[3]),
        pltpu.make_async_copy(start_hbm, start, arg_sem.at[4]),
        pltpu.make_async_copy(along_off_hbm, along_off, arg_sem.at[5]),
        pltpu.make_async_copy(across_off_hbm, across_off, arg_sem.at[6]),
    ]
    for copy in early:
        copy.start()
    for c in range(EARLY_CHUNKS):
        cube_starts(c)

    barrier = pltpu.get_barrier_semaphore()
    pl.semaphore_signal(barrier, inc=1, device_id=other, device_id_type=MESH)
    pl.semaphore_signal(barrier, inc=1, device_id=partner, device_id_type=MESH)

    @pl.when(has_ahead)
    def _():
        pl.semaphore_signal(barrier, inc=1, device_id={"line": ahead}, device_id_type=MESH)

    @pl.when(has_behind)
    def _():
        pl.semaphore_signal(barrier, inc=1, device_id={"line": behind}, device_id_type=MESH)

    tall, wide = 2 * half * ROWS, bands * ROWS
    spread[...] = (iota((128, wide), 1) // ROWS == iota((128, wide), 0)).astype(BF16)
    equal = iota((tall, wide), 0) % ROWS == iota((tall, wide), 1) % ROWS
    same[...] = jnp.where(equal, 1.0, 0.0).astype(BF16)

    for copy in early:
        copy.wait()
    for c in range(EARLY_CHUNKS, len(chunks)):
        cube_starts(c)
    along_copy.start()
    across_copy.start()
    seen_copy.start()

    lane = core * bands + iota((ms, 128), 1)
    row = iota((ms, 128), 0)
    first = jnp.zeros((ms, 128), jnp.int32)
    for m in range(ms):
        first = jnp.where(row == m, start[m], first)
    slot = lane - SPB * first
    weights = values[...].astype(F32)
    response = jnp.zeros((ms, 128), F32)
    for j in range(2 * SPB):
        response = jnp.where(slot == j, weights[:, j : j + 1], response)
    picks = iota((tall, ms), 0) // ROWS
    owner = jnp.where(picks < half, theirs * half + picks, mine * half + picks - half)
    choose = (owner == iota((tall, ms), 1)).astype(BF16)
    per_row = jnp.dot(choose, response.astype(BF16), preferred_element_type=F32).astype(BF16)
    spread_rows = jnp.dot(per_row, spread[...], preferred_element_type=F32)
    folder[...] = spread_rows.astype(BF16) * same[...]

    peers = 2 + has_ahead.astype(jnp.int32) + has_behind.astype(jnp.int32)

    def place(k, block, g, value):
        high, low = halves(value)
        stack[k, pl.ds(2 * block * lines + g * ROWS, ROWS), :] = high
        stack[k, pl.ds((2 * block + 1) * lines + g * ROWS, ROWS), :] = low

    def fold(c):
        first_group, size = chunks[c]
        cube_wait(c)
        for g in range(first_group, first_group + size):
            block = field[g].reshape(wide, columns)
            part = jnp.dot(folder[...], block, preferred_element_type=F32)
            part = part.reshape(2 * half, ROWS, columns)
            given[g] = part[:half]
            own[g] = part[half:]

    def encode(c):
        first_group, size = chunks[c]
        give_copy(chunks[c], c).wait_recv()
        span = pl.ds(first_group, size)
        code, unit = coded_of(own[span] + got[span], (0, 1, 2))
        coded[span] = code
        scale[c] = unit[0, 0]
        near_scale_copy((c, 1), c).start()
        for h, (at, *hop) in enumerate(hops):
            if at == c:
                near_copy(hop, h).start()

        @pl.when(has_behind)
        def _():
            @counted
            def _(count):
                for copy in side_copies(chunks[c], (c, 1), int(c == last_chunk), count):
                    copy.start()

        for g in range(first_group, first_group + size):
            value = own[g] + got[g]
            for k in range(half):
                place(k, 0, g, value[k])

    for step, c in ORDER:
        if step == FOLD:
            fold(c)
            if c == 0:
                pl.semaphore_wait(barrier, peers)
            give_copy(chunks[c], c).start()
        else:
            encode(c)

    along_copy.wait()
    across_copy.wait()
    before, after = (picked(along, along_off, -1), picked(along, along_off, 1))
    middle = picked(along, along_off, 0)
    near_tap = jnp.where(even, after, before).astype(BF16)
    far_tap = jnp.where(even, before, after).astype(BF16)
    middle = middle.astype(BF16)
    taps[...] = jnp.concatenate([middle, middle, near_tap, near_tap, far_tap, far_tap], axis=1)
    partner_taps[...] = jnp.concatenate([far_tap, far_tap, near_tap, near_tap], axis=1)
    count = columns // BLK
    mixer[...] = jnp.zeros(mixer.shape, BF16)
    for shift in (-1, 0, 1):
        turned = jnp.transpose(picked(across, across_off, shift)).astype(BF16)
        for j in range(count):
            if 0 <= j + shift < count:
                for part in range(2):
                    top = part * columns + (j + shift) * BLK
                    mixer[top : top + BLK, j * BLK : (j + 1) * BLK] = turned

    @pl.when(jnp.logical_not(has_behind))
    def _():
        stack[0:direct, 4 * lines : 6 * lines, :] = jnp.zeros((direct, 2 * lines, columns), BF16)

    @pl.when(jnp.logical_not(has_ahead))
    def _():
        stack[direct:half, 2 * lines : 4 * lines, :] = jnp.zeros((relayed, 2 * lines, columns), BF16)

    def mixed(smooth):
        both = jnp.concatenate(halves(smooth), axis=1)
        return jnp.dot(both, mixer[...], preferred_element_type=F32)

    def take_near(h):
        c, *hop = hops[h]
        opens = hop[0] == chunks[c][0]
        if opens:
            near_scale_copy((c, 1), c).wait_recv()
        near_copy(hop, h).wait_recv()

        @pl.when(has_ahead)
        def _():
            if opens:
                far_scale_copy((c, 1), int(c == last_chunk)).start()
            far_copy(hop, int(c == last_chunk)).start()

        for g in range(hop[0], sum(hop)):
            for k in range(direct):
                place(k, 1, g, value_of(near[g, k], near_scale[c]))

    def span_groups(n):
        for c, (first_group, size) in enumerate(chunks):
            if (c == last_chunk) == bool(n):
                for g in range(first_group, first_group + size):
                    yield c, g

    def take_side(n):
        @pl.when(has_ahead)
        def _():
            @counted
            def _(count):
                for copy in side_copies(spans[n], scale_spans[n], n, count):
                    copy.wait_recv()
                for c, g in span_groups(n):
                    for r in range(count):
                        place(direct + r, 1, g, value_of(side[g, r], side_scale[c]))

    def take_far(n):
        @pl.when(has_behind)
        def _():
            far_scale_copy(scale_spans[n], n).wait_recv()
            far_copy(spans[n], n).wait_recv()
            spots = [(c, g, k) for c, g in span_groups(n) for k in range(direct)]
            full = mixed(
                jnp.concatenate([value_of(far[g, k], far_scale[c]) for c, g, k in spots], axis=0)
            )
            for spot, (c, g, k) in enumerate(spots):
                place(k, 2, g, full[spot * ROWS : (spot + 1) * ROWS])

    def make(r):
        k = direct + r

        def body():
            smooth = jnp.dot(
                partner_taps[...], stack[k, 0 : 4 * lines, :], preferred_element_type=F32
            )
            full = mixed(smooth)
            for n, (owner, top, rows) in enumerate(parts):
                if owner == r:
                    made[r, pl.ds(top, rows)], made_scale[n] = coded_of(full[top : top + rows], 0)
                    for copy in came_copies(n):
                        copy.start()

        guard(k, mine, body)

    def begin(r):
        k = direct + r

        def body():
            smooth = jnp.dot(
                taps[:, 0 : 2 * lines], stack[k, 0 : 2 * lines, :], preferred_element_type=F32
            )
            base[r] = mixed(smooth)

        guard(k, mine, body)

    def filtered(tap_columns, ks):
        first, size = tap_columns
        wide_stack = jnp.concatenate([stack[k, first : first + size, :] for k in ks], axis=1)
        smooth = jnp.dot(
            taps[:, first : first + size], wide_stack, preferred_element_type=F32
        )
        return [smooth[:, n * columns : (n + 1) * columns] for n in range(len(ks))]

    def begin_direct(ks):
        full = mixed(jnp.concatenate(filtered((0, 4 * lines), ks), axis=0))
        for n, k in enumerate(ks):
            early_sum[k] = full[n * lines : (n + 1) * lines]

    def finish_direct(ks):
        for k, value in zip(ks, filtered((4 * lines, 2 * lines), ks)):
            synthetic[mine * half + k] = early_sum[k] + value
        for k in ks:
            share_copy(mine, k, 0, lines).start()

    def finish_relayed(n):
        r, top, rows = parts[n]
        k = direct + r

        def body():
            for copy in came_copies(n):
                copy.wait_recv()
            span = pl.ds(top, rows)
            added = value_of(came[r, span], came_scale[n])
            synthetic[mine * half + k, span, :] = base[r, span, :] + added
            share_copy(mine, k, top, rows).start()

        guard(k, mine, body)

    def measure(t, carry):
        rows = pl.ds(t * ROWS, ROWS)
        level = jnp.zeros((ROWS, columns), F32)
        for m in range(ms):
            sight = seen[m, rows, :].astype(F32)
            level += sight * sight
        power_seen[rows, :] = level
        return carry

    seen_copy.wait()
    lax.fori_loop(0, groups, measure, 0)
    take_near(0)
    begin(0)
    take_near(1)
    for r in range(1, relayed):
        begin(r)
    take_near(2)
    take_side(0)
    take_side(1)
    make(0)
    take_near(3)
    make(1)
    for h in range(4, len(hops)):
        take_near(h)
    for r in range(2, relayed):
        make(r)
    teams = [range(k, min(k + TEAM, direct)) for k in range(0, direct, TEAM)]
    late = [n for n in range(len(parts)) if parts[n][0] > 0]
    for ks in teams:
        begin_direct(ks)
    take_far(0)
    for n in range(len(parts)):
        if n not in late:
            finish_relayed(n)
    take_far(1)
    for ks in teams:
        finish_direct(ks)
    for n in late:
        finish_relayed(n)
    share_all(theirs, 0).wait_recv()

    every, every_scale = (0, groups), (0, len(chunks))
    give_copy(every, 0).wait_send()
    near_copy(every, 0).wait_send()
    near_scale_copy(every_scale, 0).wait_send()

    @pl.when(has_ahead)
    def _():
        far_copy(every, 0).wait_send()
        far_scale_copy(every_scale, 0).wait_send()

    @pl.when(has_behind)
    def _():
        @counted
        def _(count):
            for copy in side_copies(every, every_scale, 0, count):
                copy.wait_send()

    def made_sent(kind):
        first, count = ((0, relayed - 1), (relayed - 1, 1))[kind]
        numbers = [n for n in range(len(parts)) if (parts[n][0] == relayed - 1) == bool(kind)]
        span, scale_span = pl.ds(first, count), pl.ds(numbers[0], len(numbers))
        remote(
            made.at[span], came.at[span], came_sent.at[0, kind], came_sem.at[0, 0], partner
        ).wait_send()
        remote(
            made_scale.at[scale_span],
            came_scale.at[scale_span],
            came_sent.at[1, kind],
            came_sem.at[1, 0],
            partner,
        ).wait_send()

    made_sent(0)
    share_all(mine, 0).wait_send()
    share_all(mine, 1).wait_send()
    share_all(theirs, 1).wait_recv()

    def last_sent():
        made_sent(1)
        share_all(mine, 2).wait_send()

    guard(half - 1, mine, last_sent)
    guard(half - 1, theirs, lambda: share_all(theirs, 2).wait_recv())


def arccos(x):
    size = jnp.abs(x)
    big = size > 0.5
    square = jnp.where(big, 0.5 - 0.5 * size, size * size)
    root = jnp.where(big, jnp.sqrt(square), size)
    poly = 4.2163199048e-2
    for term in (2.4181311049e-2, 4.5470025998e-2, 7.4953002686e-2, 1.6666752422e-1):
        poly = poly * square + term
    arc = root + root * square * poly
    angle = jnp.where(big, 2.0 * arc, 0.5 * math.pi - arc)
    return jnp.where(x < 0.0, math.pi - angle, angle)


def finish_kernel(synthetic, seen, power_seen, synthetic_out, angles_out, angles, sem):
    copy = pltpu.make_async_copy(synthetic, synthetic_out, sem.at[0])
    copy.start()

    def angle(t, carry):
        rows = pl.ds(t * ROWS, ROWS)
        inner = power = jnp.zeros((ROWS, angles.shape[1]), F32)
        for m in range(synthetic.shape[0]):
            value = synthetic[m, rows, :]
            inner += value * seen[m, rows, :].astype(F32)
            power += value * value
        norm = jnp.maximum(jnp.sqrt(power) * jnp.sqrt(power_seen[rows, :]), 1.0)
        angles[rows, :] = arccos(jnp.clip(inner / norm, -1.0, 1.0))
        return carry

    lax.fori_loop(0, angles.shape[0] // ROWS, angle, 0, unroll=True)
    last = pltpu.make_async_copy(angles, angles_out, sem.at[1])
    last.start()
    copy.wait()
    last.wait()


def on_device(
    cube,
    observed,
    along_kernels,
    along_offsets,
    across_kernels,
    across_offsets,
    resp_start,
    resp_values,
):
    bands, lines, columns = cube.shape
    ms = observed.shape[0]
    cores = lax.axis_size("band")
    line_size = lax.axis_size("line")
    assert cores == 2 and line_size % 2 == 0 and lines == BLK and bands <= 128
    half = -(-ms // cores)
    direct = (half + 1) // 2
    relayed = half - direct
    groups = lines // ROWS
    assert sum(CHUNKS) == groups and len(PARTS) == relayed and relayed > 1
    sizes = (bands, lines, columns, ms, half, direct, line_size)
    hbm = pl.BlockSpec(memory_space=pltpu.HBM)
    vmem = pl.BlockSpec(memory_space=pltpu.VMEM)
    dma = pltpu.SemaphoreType.DMA
    results = pl.pallas_call(
        functools.partial(kernel, sizes),
        out_shape=(
            pltpu.VMEM((ms, lines, columns), F32),
            pltpu.VMEM((ms, lines, columns), BF16),
            pltpu.VMEM((lines, columns), F32),
        ),
        in_specs=[hbm] * 8,
        out_specs=(vmem,) * 3,
        scratch_shapes=[
            pltpu.VMEM((2 * half * ROWS, bands * ROWS), BF16),
            pltpu.VMEM((128, bands * ROWS), BF16),
            pltpu.VMEM((2 * half * ROWS, bands * ROWS), BF16),
            pltpu.VMEM((groups, bands, ROWS, columns), BF16),
            pltpu.VMEM((3, BLK, BLK), BF16),
            pltpu.VMEM((3, BLK, BLK), BF16),
            pltpu.VMEM((BLK, 6 * BLK), BF16),
            pltpu.VMEM((BLK, 4 * BLK), BF16),
            pltpu.VMEM((2 * columns, columns), BF16),
            pltpu.VMEM((groups, half, ROWS, columns), F32),
            pltpu.VMEM((groups, half, ROWS, columns), F32),
            pltpu.VMEM((groups, half, ROWS, columns), F32),
            pltpu.VMEM((groups, half, ROWS, columns), I16),
            pltpu.VMEM((len(CHUNKS), 1, columns), F32),
            pltpu.VMEM((groups, direct, ROWS, columns), I16),
            pltpu.VMEM((len(CHUNKS), 1, columns), F32),
            pltpu.VMEM((groups, direct, ROWS, columns), I16),
            pltpu.VMEM((len(CHUNKS), 1, columns), F32),
            pltpu.VMEM((groups, relayed, ROWS, columns), I16),
            pltpu.VMEM((len(CHUNKS), 1, columns), F32),
            pltpu.VMEM((half, 6 * lines, columns), BF16),
            pltpu.VMEM((relayed, lines, columns), F32),
            pltpu.VMEM((direct, lines, columns), F32),
            pltpu.VMEM((relayed, lines, columns), I16),
            pltpu.VMEM((sum(PARTS), 1, columns), F32),
            pltpu.VMEM((relayed, lines, columns), I16),
            pltpu.VMEM((sum(PARTS), 1, columns), F32),
            pltpu.VMEM(resp_values.shape, BF16),
            pltpu.SMEM(along_offsets.shape, jnp.int32),
            pltpu.SMEM(across_offsets.shape, jnp.int32),
            pltpu.SMEM(resp_start.shape, jnp.int32),
            dma((len(CHUNKS),)),
            dma((7,)),
            dma((1,)),
            dma((len(CHUNKS),)),
            dma((2,)),
            dma((2 * len(CHUNKS) + CHUNKS[-1] - 1,)),
            dma((2,)),
            dma((2, 2)),
            dma((2,)),
            dma((2, 2)),
            dma((2, 2)),
            dma((2, sum(PARTS))),
            dma((3,)),
            dma((3,)),
        ],
        compiler_params=pltpu.CompilerParams(
            collective_id=0, has_side_effects=True, vmem_limit_bytes=48_000_000
        ),
    )(
        *(
            pltpu.with_memory_space_constraint(value, pltpu.HBM)
            for value in (
                cube,
                observed,
                along_kernels,
                across_kernels,
                resp_values,
                along_offsets,
                across_offsets,
                resp_start,
            )
        )
    )
    return pl.pallas_call(
        finish_kernel,
        out_shape=(
            jax.ShapeDtypeStruct((ms, lines, columns), F32),
            jax.ShapeDtypeStruct((lines, columns), F32),
        ),
        in_specs=[vmem] * 3,
        out_specs=(hbm, hbm),
        scratch_shapes=[pltpu.VMEM((lines, columns), F32), dma((2,))],
        compiler_params=pltpu.CompilerParams(vmem_limit_bytes=8_000_000),
    )(*(pltpu.with_memory_space_constraint(value, pltpu.VMEM) for value in results))


def solution(mesh):
    placed = (
        P("band", ("slab", "line"), None),
        P(None, ("slab", "line"), None),
        P(),
        P(),
        P(),
        P(),
        P(),
        P(),
    )
    return jax.shard_map(
        on_device,
        mesh=mesh,
        in_specs=placed,
        out_specs=(P(None, ("slab", "line"), None), P(("slab", "line"), None)),
        check_vma=False,
    )
```

```python
import functools
import math

import jax
import jax.numpy as jnp
from jax import lax
from jax.experimental import pallas as pl
from jax.experimental.pallas import tpu as pltpu
from jax.sharding import PartitionSpec as P

BLK = 128
SPB = 10
ROWS = 16
EARLY_CHUNKS = 3
CHUNKS = (1, 1, 2, 2, 2)
FOLD, CODE = 0, 1
ORDER = (
    (FOLD, 0),
    (FOLD, 1),
    (FOLD, 2),
    (CODE, 0),
    (CODE, 1),
    (FOLD, 3),
    (CODE, 2),
    (FOLD, 4),
    (CODE, 3),
    (CODE, 4),
)
PARTS = (1, 1, 1)
TEAM = 4
MESH = pl.DeviceIdType.MESH
F32 = jnp.float32
BF16 = jnp.bfloat16
I16 = jnp.int16
PEAK = 32767.0


def halves(value):
    high = value.astype(BF16)
    low = (value - high.astype(F32)).astype(BF16)
    return high, low


def coded_of(value, axes):
    peak = jnp.max(jnp.abs(value), axis=axes, keepdims=True)
    inverse = jnp.where(peak > 0.0, PEAK / jnp.maximum(peak, 1e-30), 0.0)
    code = jnp.round(value * inverse).astype(jnp.int32).astype(I16)
    return code, peak * (1.0 / PEAK)


def value_of(code, scale):
    return code.astype(jnp.int32).astype(F32) * scale


def picked(kernels, offsets, shift):
    total = None
    for k in range(3):
        term = jnp.where(offsets[k] == shift, kernels[k].astype(F32), 0.0)
        total = term if total is None else total + term
    return total


def iota(shape, dim):
    return lax.broadcasted_iota(jnp.int32, shape, dim)


def kernel(
    sizes,
    cube,
    observed,
    along_hbm,
    across_hbm,
    values_hbm,
    along_off_hbm,
    across_off_hbm,
    start_hbm,
    synthetic,
    seen,
    power_seen,
    folder,
    spread,
    same,
    field,
    along,
    across,
    taps,
    partner_taps,
    mixer,
    given,
    own,
    got,
    coded,
    scale,
    near,
    near_scale,
    far,
    far_scale,
    side,
    side_scale,
    stack,
    base,
    early_sum,
    made,
    made_scale,
    came,
    came_scale,
    values,
    along_off,
    across_off,
    start,
    cube_sem,
    arg_sem,
    give_sent,
    give_sem,
    near_sent,
    near_sem,
    far_sent,
    far_sem,
    side_sent,
    side_sem,
    came_sent,
    came_sem,
    share_sent,
    share_sem,
):
    bands, lines, columns, ms, half, direct, line_size = sizes
    groups = lines // ROWS
    relayed = half - direct
    core = lax.axis_index("band")
    index = lax.axis_index("line")
    mine, theirs = 1 - core, core
    other = {"band": 1 - core}
    even = index % 2 == 0
    partner = {"line": index + 1 - 2 * (index % 2)}
    step = 2 - 4 * (index % 2)
    ahead, behind = index + step, index - step
    has_ahead = jnp.logical_and(ahead >= 0, ahead < line_size)
    has_behind = jnp.logical_and(behind >= 0, behind < line_size)

    chunks = []
    for size in CHUNKS:
        begin_at = chunks[-1][0] + chunks[-1][1] if chunks else 0
        chunks.append((begin_at, size))
    last_chunk = len(chunks) - 1
    spans = ((0, chunks[-1][0]), chunks[-1])
    scale_spans = ((0, last_chunk), (last_chunk, 1))
    hops = [(c, *chunks[c]) for c in range(last_chunk)]
    hops += [(last_chunk, g, 1) for g in range(chunks[-1][0], groups)]
    parts = []
    for r, count in enumerate(PARTS):
        for piece in range(count):
            parts.append((r, piece * (lines // count), lines // count))

    def remote(src, dst, sent, sem, device):
        return pltpu.make_async_remote_copy(
            src_ref=src,
            dst_ref=dst,
            send_sem=sent,
            recv_sem=sem,
            device_id=device,
            device_id_type=MESH,
        )

    def cube_copy(g, c):
        return pltpu.make_async_copy(
            cube.at[:, pl.ds(g * ROWS, ROWS), :], field.at[g], cube_sem.at[c]
        )

    def cube_starts(c):
        first_group, size = chunks[c]
        for g in range(first_group, first_group + size):
            cube_copy(g, c).start()

    def cube_wait(c):
        ref = field.at[pl.ds(*chunks[c])]
        pltpu.make_async_copy(ref, ref, cube_sem.at[c]).wait()

    def give_copy(span, c):
        span = pl.ds(*span)
        return remote(given.at[span], got.at[span], give_sent.at[0], give_sem.at[c], other)

    def near_copy(span, h):
        span = pl.ds(*span)
        return remote(
            coded.at[span, pl.ds(0, direct)], near.at[span], near_sent.at[0], near_sem.at[h], partner
        )

    def near_scale_copy(span, c):
        span = pl.ds(*span)
        return remote(
            scale.at[span], near_scale.at[span], near_sent.at[1], near_sem.at[len(hops) + c], partner
        )

    def far_copy(span, n):
        span = pl.ds(*span)
        return remote(near.at[span], far.at[span], far_sent.at[0], far_sem.at[0, n], {"line": ahead})

    def far_scale_copy(span, n):
        span = pl.ds(*span)
        return remote(
            near_scale.at[span],
            far_scale.at[span],
            far_sent.at[1],
            far_sem.at[1, n],
            {"line": ahead},
        )

    def side_copies(span, scale_span, n, count):
        span, scale_span = pl.ds(*span), pl.ds(*scale_span)
        device = {"line": behind}
        return (
            remote(
                coded.at[span, pl.ds(direct, count)],
                side.at[span, pl.ds(0, count)],
                side_sent.at[0],
                side_sem.at[0, n],
                device,
            ),
            remote(
                scale.at[scale_span],
                side_scale.at[scale_span],
                side_sent.at[1],
                side_sem.at[1, n],
                device,
            ),
        )

    def came_copies(n):
        r, top, rows = parts[n]
        kind = int(r == relayed - 1)
        return (
            remote(
                made.at[r, pl.ds(top, rows)],
                came.at[r, pl.ds(top, rows)],
                came_sent.at[0, kind],
                came_sem.at[0, n],
                partner,
            ),
            remote(
                made_scale.at[n], came_scale.at[n], came_sent.at[1, kind], came_sem.at[1, n], partner
            ),
        )

    def share_copy(place, k, top, rows):
        kind = int(k >= direct) + int(k == half - 1)
        ref = synthetic.at[place * half + k, pl.ds(top, rows)]
        return remote(ref, ref, share_sent.at[kind], share_sem.at[kind], other)

    def share_all(place, kind):
        first_k, count = ((0, direct), (direct, relayed - 1), (half - 1, 1))[kind]
        ref = synthetic.at[pl.ds(place * half + first_k, count)]
        return remote(ref, ref, share_sent.at[kind], share_sem.at[kind], other)

    def counted(body):
        if 2 * half == ms:
            body(relayed)
        else:
            whole = mine * half + half <= ms
            pl.when(whole)(lambda: body(relayed))
            pl.when(jnp.logical_not(whole))(lambda: body(relayed - 1))

    def guard(k, place, body):
        if half + k < ms:
            body()
        else:
            pl.when(place * half + k < ms)(body)

    along_copy = pltpu.make_async_copy(along_hbm, along, arg_sem.at[0])
    across_copy = pltpu.make_async_copy(across_hbm, across, arg_sem.at[1])
    seen_copy = pltpu.make_async_copy(observed, seen, arg_sem.at[2])
    early = [
        pltpu.make_async_copy(values_hbm, values, arg_sem.at[3]),
        pltpu.make_async_copy(start_hbm, start, arg_sem.at[4]),
        pltpu.make_async_copy(along_off_hbm, along_off, arg_sem.at[5]),
        pltpu.make_async_copy(across_off_hbm, across_off, arg_sem.at[6]),
    ]
    for copy in early:
        copy.start()
    for c in range(EARLY_CHUNKS):
        cube_starts(c)

    barrier = pltpu.get_barrier_semaphore()
    pl.semaphore_signal(barrier, inc=1, device_id=other, device_id_type=MESH)
    pl.semaphore_signal(barrier, inc=1, device_id=partner, device_id_type=MESH)

    @pl.when(has_ahead)
    def _():
        pl.semaphore_signal(barrier, inc=1, device_id={"line": ahead}, device_id_type=MESH)

    @pl.when(has_behind)
    def _():
        pl.semaphore_signal(barrier, inc=1, device_id={"line": behind}, device_id_type=MESH)

    tall, wide = 2 * half * ROWS, bands * ROWS
    spread[...] = (iota((128, wide), 1) // ROWS == iota((128, wide), 0)).astype(BF16)
    equal = iota((tall, wide), 0) % ROWS == iota((tall, wide), 1) % ROWS
    same[...] = jnp.where(equal, 1.0, 0.0).astype(BF16)

    for copy in early:
        copy.wait()
    for c in range(EARLY_CHUNKS, len(chunks)):
        cube_starts(c)

    lane = core * bands + iota((ms, 128), 1)
    row = iota((ms, 128), 0)
    first = jnp.zeros((ms, 128), jnp.int32)
    for m in range(ms):
        first = jnp.where(row == m, start[m], first)
    slot = lane - SPB * first
    weights = values[...].astype(F32)
    response = jnp.zeros((ms, 128), F32)
    for j in range(2 * SPB):
        response = jnp.where(slot == j, weights[:, j : j + 1], response)
    picks = iota((tall, ms), 0) // ROWS
    owner = jnp.where(picks < half, theirs * half + picks, mine * half + picks - half)
    choose = (owner == iota((tall, ms), 1)).astype(BF16)
    per_row = jnp.dot(choose, response.astype(BF16), preferred_element_type=F32).astype(BF16)
    spread_rows = jnp.dot(per_row, spread[...], preferred_element_type=F32)
    folder[...] = spread_rows.astype(BF16) * same[...]

    peers = 2 + has_ahead.astype(jnp.int32) + has_behind.astype(jnp.int32)

    def place(k, block, g, value):
        high, low = halves(value)
        stack[k, pl.ds(2 * block * lines + g * ROWS, ROWS), :] = high
        stack[k, pl.ds((2 * block + 1) * lines + g * ROWS, ROWS), :] = low

    def fold(c):
        first_group, size = chunks[c]
        cube_wait(c)
        for g in range(first_group, first_group + size):
            block = field[g].reshape(wide, columns)
            part = jnp.dot(folder[...], block, preferred_element_type=F32)
            part = part.reshape(2 * half, ROWS, columns)
            given[g] = part[:half]
            own[g] = part[half:]

    def encode(c):
        first_group, size = chunks[c]
        give_copy(chunks[c], c).wait_recv()
        span = pl.ds(first_group, size)
        code, unit = coded_of(own[span] + got[span], (0, 1, 2))
        coded[span] = code
        scale[c] = unit[0, 0]
        near_scale_copy((c, 1), c).start()
        for h, (at, *hop) in enumerate(hops):
            if at == c:
                near_copy(hop, h).start()

        @pl.when(has_behind)
        def _():
            @counted
            def _(count):
                for copy in side_copies(chunks[c], (c, 1), int(c == last_chunk), count):
                    copy.start()

        for g in range(first_group, first_group + size):
            value = own[g] + got[g]
            for k in range(half):
                place(k, 0, g, value[k])

    for step, c in ORDER:
        if step == FOLD:
            fold(c)
            if c == 0:
                pl.semaphore_wait(barrier, peers)
            give_copy(chunks[c], c).start()
            if c == last_chunk - 1:
                along_copy.start()
                across_copy.start()
                seen_copy.start()
        else:
            encode(c)

    along_copy.wait()
    across_copy.wait()
    before, after = (picked(along, along_off, -1), picked(along, along_off, 1))
    middle = picked(along, along_off, 0)
    near_tap = jnp.where(even, after, before).astype(BF16)
    far_tap = jnp.where(even, before, after).astype(BF16)
    middle = middle.astype(BF16)
    taps[...] = jnp.concatenate([middle, middle, near_tap, near_tap, far_tap, far_tap], axis=1)
    partner_taps[...] = jnp.concatenate([far_tap, far_tap, near_tap, near_tap], axis=1)
    count = columns // BLK
    mixer[...] = jnp.zeros(mixer.shape, BF16)
    for shift in (-1, 0, 1):
        turned = jnp.transpose(picked(across, across_off, shift)).astype(BF16)
        for j in range(count):
            if 0 <= j + shift < count:
                for part in range(2):
                    top = part * columns + (j + shift) * BLK
                    mixer[top : top + BLK, j * BLK : (j + 1) * BLK] = turned

    @pl.when(jnp.logical_not(has_behind))
    def _():
        stack[0:direct, 4 * lines : 6 * lines, :] = jnp.zeros((direct, 2 * lines, columns), BF16)

    @pl.when(jnp.logical_not(has_ahead))
    def _():
        stack[direct:half, 2 * lines : 4 * lines, :] = jnp.zeros((relayed, 2 * lines, columns), BF16)

    def mixed(smooth):
        both = jnp.concatenate(halves(smooth), axis=1)
        return jnp.dot(both, mixer[...], preferred_element_type=F32)

    def take_near(h):
        c, *hop = hops[h]
        opens = hop[0] == chunks[c][0]
        if opens:
            near_scale_copy((c, 1), c).wait_recv()
        near_copy(hop, h).wait_recv()

        @pl.when(has_ahead)
        def _():
            if opens:
                far_scale_copy((c, 1), int(c == last_chunk)).start()
            far_copy(hop, int(c == last_chunk)).start()

        for g in range(hop[0], sum(hop)):
            for k in range(direct):
                place(k, 1, g, value_of(near[g, k], near_scale[c]))

    def span_groups(n):
        for c, (first_group, size) in enumerate(chunks):
            if (c == last_chunk) == bool(n):
                for g in range(first_group, first_group + size):
                    yield c, g

    def take_side(n):
        @pl.when(has_ahead)
        def _():
            @counted
            def _(count):
                for copy in side_copies(spans[n], scale_spans[n], n, count):
                    copy.wait_recv()
                for c, g in span_groups(n):
                    for r in range(count):
                        place(direct + r, 1, g, value_of(side[g, r], side_scale[c]))

    def take_far(n):
        @pl.when(has_behind)
        def _():
            far_scale_copy(scale_spans[n], n).wait_recv()
            far_copy(spans[n], n).wait_recv()
            spots = [(c, g, k) for c, g in span_groups(n) for k in range(direct)]
            full = mixed(
                jnp.concatenate([value_of(far[g, k], far_scale[c]) for c, g, k in spots], axis=0)
            )
            for spot, (c, g, k) in enumerate(spots):
                place(k, 2, g, full[spot * ROWS : (spot + 1) * ROWS])

    def make(r):
        k = direct + r

        def body():
            smooth = jnp.dot(
                partner_taps[...], stack[k, 0 : 4 * lines, :], preferred_element_type=F32
            )
            full = mixed(smooth)
            for n, (owner, top, rows) in enumerate(parts):
                if owner == r:
                    made[r, pl.ds(top, rows)], made_scale[n] = coded_of(full[top : top + rows], 0)
                    for copy in came_copies(n):
                        copy.start()

        guard(k, mine, body)

    def begin(r):
        k = direct + r

        def body():
            smooth = jnp.dot(
                taps[:, 0 : 2 * lines], stack[k, 0 : 2 * lines, :], preferred_element_type=F32
            )
            base[r] = mixed(smooth)

        guard(k, mine, body)

    def filtered(tap_columns, ks):
        first, size = tap_columns
        wide_stack = jnp.concatenate([stack[k, first : first + size, :] for k in ks], axis=1)
        smooth = jnp.dot(
            taps[:, first : first + size], wide_stack, preferred_element_type=F32
        )
        return [smooth[:, n * columns : (n + 1) * columns] for n in range(len(ks))]

    def begin_direct(ks):
        full = mixed(jnp.concatenate(filtered((0, 4 * lines), ks), axis=0))
        for n, k in enumerate(ks):
            early_sum[k] = full[n * lines : (n + 1) * lines]

    def finish_direct(ks):
        for k, value in zip(ks, filtered((4 * lines, 2 * lines), ks)):
            synthetic[mine * half + k] = early_sum[k] + value
        for k in ks:
            share_copy(mine, k, 0, lines).start()

    def finish_relayed(n):
        r, top, rows = parts[n]
        k = direct + r

        def body():
            for copy in came_copies(n):
                copy.wait_recv()
            span = pl.ds(top, rows)
            added = value_of(came[r, span], came_scale[n])
            synthetic[mine * half + k, span, :] = base[r, span, :] + added
            share_copy(mine, k, top, rows).start()

        guard(k, mine, body)

    def measure(t, carry):
        rows = pl.ds(t * ROWS, ROWS)
        level = jnp.zeros((ROWS, columns), F32)
        for m in range(ms):
            sight = seen[m, rows, :].astype(F32)
            level += sight * sight
        power_seen[rows, :] = level
        return carry

    seen_copy.wait()
    lax.fori_loop(0, groups, measure, 0)
    take_near(0)
    begin(0)
    take_near(1)
    for r in range(1, relayed):
        begin(r)
    take_near(2)
    take_side(0)
    take_side(1)
    make(0)
    take_near(3)
    make(1)
    for h in range(4, len(hops)):
        take_near(h)
    for r in range(2, relayed):
        make(r)
    teams = [range(k, min(k + TEAM, direct)) for k in range(0, direct, TEAM)]
    late = [n for n in range(len(parts)) if parts[n][0] > 0]
    for ks in teams:
        begin_direct(ks)
    take_far(0)
    for n in range(len(parts)):
        if n not in late:
            finish_relayed(n)
    take_far(1)
    for ks in teams:
        finish_direct(ks)
    for n in late:
        finish_relayed(n)
    share_all(theirs, 0).wait_recv()

    every, every_scale = (0, groups), (0, len(chunks))
    give_copy(every, 0).wait_send()
    near_copy(every, 0).wait_send()
    near_scale_copy(every_scale, 0).wait_send()

    @pl.when(has_ahead)
    def _():
        far_copy(every, 0).wait_send()
        far_scale_copy(every_scale, 0).wait_send()

    @pl.when(has_behind)
    def _():
        @counted
        def _(count):
            for copy in side_copies(every, every_scale, 0, count):
                copy.wait_send()

    def made_sent(kind):
        first, count = ((0, relayed - 1), (relayed - 1, 1))[kind]
        numbers = [n for n in range(len(parts)) if (parts[n][0] == relayed - 1) == bool(kind)]
        span, scale_span = pl.ds(first, count), pl.ds(numbers[0], len(numbers))
        remote(
            made.at[span], came.at[span], came_sent.at[0, kind], came_sem.at[0, 0], partner
        ).wait_send()
        remote(
            made_scale.at[scale_span],
            came_scale.at[scale_span],
            came_sent.at[1, kind],
            came_sem.at[1, 0],
            partner,
        ).wait_send()

    made_sent(0)
    share_all(mine, 0).wait_send()
    share_all(mine, 1).wait_send()
    share_all(theirs, 1).wait_recv()

    def last_sent():
        made_sent(1)
        share_all(mine, 2).wait_send()

    guard(half - 1, mine, last_sent)
    guard(half - 1, theirs, lambda: share_all(theirs, 2).wait_recv())


def arccos(x):
    size = jnp.abs(x)
    big = size > 0.5
    square = jnp.where(big, 0.5 - 0.5 * size, size * size)
    root = jnp.where(big, jnp.sqrt(square), size)
    poly = 4.2163199048e-2
    for term in (2.4181311049e-2, 4.5470025998e-2, 7.4953002686e-2, 1.6666752422e-1):
        poly = poly * square + term
    arc = root + root * square * poly
    angle = jnp.where(big, 2.0 * arc, 0.5 * math.pi - arc)
    return jnp.where(x < 0.0, math.pi - angle, angle)


def finish_kernel(synthetic, seen, power_seen, synthetic_out, angles_out, angles, sem):
    copy = pltpu.make_async_copy(synthetic, synthetic_out, sem.at[0])
    copy.start()

    def angle(t, carry):
        rows = pl.ds(t * ROWS, ROWS)
        inner = power = jnp.zeros((ROWS, angles.shape[1]), F32)
        for m in range(synthetic.shape[0]):
            value = synthetic[m, rows, :]
            inner += value * seen[m, rows, :].astype(F32)
            power += value * value
        norm = jnp.maximum(jnp.sqrt(power) * jnp.sqrt(power_seen[rows, :]), 1.0)
        angles[rows, :] = arccos(jnp.clip(inner / norm, -1.0, 1.0))
        return carry

    lax.fori_loop(0, angles.shape[0] // ROWS, angle, 0, unroll=True)
    last = pltpu.make_async_copy(angles, angles_out, sem.at[1])
    last.start()
    copy.wait()
    last.wait()


def on_device(
    cube,
    observed,
    along_kernels,
    along_offsets,
    across_kernels,
    across_offsets,
    resp_start,
    resp_values,
):
    bands, lines, columns = cube.shape
    ms = observed.shape[0]
    cores = lax.axis_size("band")
    line_size = lax.axis_size("line")
    assert cores == 2 and line_size % 2 == 0 and lines == BLK and bands <= 128
    half = -(-ms // cores)
    direct = (half + 1) // 2
    relayed = half - direct
    groups = lines // ROWS
    assert sum(CHUNKS) == groups and len(PARTS) == relayed and relayed > 1
    sizes = (bands, lines, columns, ms, half, direct, line_size)
    hbm = pl.BlockSpec(memory_space=pltpu.HBM)
    vmem = pl.BlockSpec(memory_space=pltpu.VMEM)
    dma = pltpu.SemaphoreType.DMA
    results = pl.pallas_call(
        functools.partial(kernel, sizes),
        out_shape=(
            pltpu.VMEM((ms, lines, columns), F32),
            pltpu.VMEM((ms, lines, columns), BF16),
            pltpu.VMEM((lines, columns), F32),
        ),
        in_specs=[hbm] * 8,
        out_specs=(vmem,) * 3,
        scratch_shapes=[
            pltpu.VMEM((2 * half * ROWS, bands * ROWS), BF16),
            pltpu.VMEM((128, bands * ROWS), BF16),
            pltpu.VMEM((2 * half * ROWS, bands * ROWS), BF16),
            pltpu.VMEM((groups, bands, ROWS, columns), BF16),
            pltpu.VMEM((3, BLK, BLK), BF16),
            pltpu.VMEM((3, BLK, BLK), BF16),
            pltpu.VMEM((BLK, 6 * BLK), BF16),
            pltpu.VMEM((BLK, 4 * BLK), BF16),
            pltpu.VMEM((2 * columns, columns), BF16),
            pltpu.VMEM((groups, half, ROWS, columns), F32),
            pltpu.VMEM((groups, half, ROWS, columns), F32),
            pltpu.VMEM((groups, half, ROWS, columns), F32),
            pltpu.VMEM((groups, half, ROWS, columns), I16),
            pltpu.VMEM((len(CHUNKS), 1, columns), F32),
            pltpu.VMEM((groups, direct, ROWS, columns), I16),
            pltpu.VMEM((len(CHUNKS), 1, columns), F32),
            pltpu.VMEM((groups, direct, ROWS, columns), I16),
            pltpu.VMEM((len(CHUNKS), 1, columns), F32),
            pltpu.VMEM((groups, relayed, ROWS, columns), I16),
            pltpu.VMEM((len(CHUNKS), 1, columns), F32),
            pltpu.VMEM((half, 6 * lines, columns), BF16),
            pltpu.VMEM((relayed, lines, columns), F32),
            pltpu.VMEM((direct, lines, columns), F32),
            pltpu.VMEM((relayed, lines, columns), I16),
            pltpu.VMEM((sum(PARTS), 1, columns), F32),
            pltpu.VMEM((relayed, lines, columns), I16),
            pltpu.VMEM((sum(PARTS), 1, columns), F32),
            pltpu.VMEM(resp_values.shape, BF16),
            pltpu.SMEM(along_offsets.shape, jnp.int32),
            pltpu.SMEM(across_offsets.shape, jnp.int32),
            pltpu.SMEM(resp_start.shape, jnp.int32),
            dma((len(CHUNKS),)),
            dma((7,)),
            dma((1,)),
            dma((len(CHUNKS),)),
            dma((2,)),
            dma((2 * len(CHUNKS) + CHUNKS[-1] - 1,)),
            dma((2,)),
            dma((2, 2)),
            dma((2,)),
            dma((2, 2)),
            dma((2, 2)),
            dma((2, sum(PARTS))),
            dma((3,)),
            dma((3,)),
        ],
        compiler_params=pltpu.CompilerParams(
            collective_id=0, has_side_effects=True, vmem_limit_bytes=48_000_000
        ),
    )(
        *(
            pltpu.with_memory_space_constraint(value, pltpu.HBM)
            for value in (
                cube,
                observed,
                along_kernels,
                across_kernels,
                resp_values,
                along_offsets,
                across_offsets,
                resp_start,
            )
        )
    )
    return pl.pallas_call(
        finish_kernel,
        out_shape=(
            jax.ShapeDtypeStruct((ms, lines, columns), F32),
            jax.ShapeDtypeStruct((lines, columns), F32),
        ),
        in_specs=[vmem] * 3,
        out_specs=(hbm, hbm),
        scratch_shapes=[pltpu.VMEM((lines, columns), F32), dma((2,))],
        compiler_params=pltpu.CompilerParams(vmem_limit_bytes=8_000_000),
    )(*(pltpu.with_memory_space_constraint(value, pltpu.VMEM) for value in results))


def solution(mesh):
    placed = (
        P("band", ("slab", "line"), None),
        P(None, ("slab", "line"), None),
        P(),
        P(),
        P(),
        P(),
        P(),
        P(),
    )
    return jax.shard_map(
        on_device,
        mesh=mesh,
        in_specs=placed,
        out_specs=(P(None, ("slab", "line"), None), P(("slab", "line"), None)),
        check_vma=False,
    )
```
